512 devices in a mesh: tf: 32 (over x, y, core), bl: 16 (over z).
Axes of the slice: x: 4, y: 4, z: 16, core: 2. Of those that a mesh axis runs over, the one named last changes fastest.
Arguments:
- gains: float32 [2, 64, 1024], P(None, 'tf', 'bl'), may hold values from -5 to 5
- gain_tan: float32 [2, 64, 1024], P(None, 'tf', 'bl'), may hold values from -6 to 6
- group_vis: float32 [2, 64, 1984], P(None, 'tf', 'bl'), may hold values from -6 to 6
- group_tan: float32 [2, 64, 1984], P(None, 'tf', 'bl'), may hold values from -6 to 6
- dish_of: int32 [1024], replicated, may hold values from 0 to 1023, each once
- group_of: int32 [1984], replicated, may hold values from 0 to 1983, each once
- block_list: int32 [528, 2], P('bl'), may hold values from 0 to 31, as said below
- weights: int32 [528, 1024], P('bl'), may hold values from 0 to 4
Outputs:
- gain_update: float32 [2, 64, 1024], P(None, 'tf', 'bl')
- group_update: float32 [2, 64, 1984], P(None, 'tf', 'bl')
The draws below stay inside these ranges and needn't reach their ends.
Inputs may be any that keep to these rules, and one draw needn't show every extreme that they name: `block_list`: each pair 0 <= r1 <= r2 < 32 stands in exactly one slot.
All inputs are finite; a program needn't handle non-finite values.
Results may differ from the reference program's by a relative error of at most 0.0003.
Values sent between devices are 32-bit elements; how exact they have to be, the bound alone decides.
No kernel may reach another device: no remote copies, remote signals or barrier semaphores. Data moves between devices by JAX's collectives and lax.ppermute only.
A program may use at most 64 MiB of HBM per device.

```python
import jax
import jax.numpy as jnp
from jax import lax

ROWS = 32
COLS = 32
NC = 64
DISHES = 1024
GROUPS = 1984
PAIRS = 528


def draw_block_list(key, part):
    inner_rank = jax.random.permutation(jax.random.fold_in(key, 41), ROWS * ROWS).astype(jnp.int32)
    flat = jnp.arange(ROWS * ROWS, dtype=jnp.int32)
    row_gap = flat // ROWS
    first_row = flat % ROWS
    valid = first_row + row_gap < ROWS
    scores = jnp.where(valid, inner_rank, 4 * ROWS * ROWS + flat)
    chosen = jnp.argsort(scores, stable=True)[:PAIRS].astype(jnp.int32)
    chosen_gap = chosen // ROWS
    chosen_first = chosen % ROWS
    return jnp.stack([chosen_first, chosen_first + chosen_gap], axis=1).astype(jnp.int32)


def touch_ends(entries, key, low, largest):
    dims = entries.shape
    spot = [jax.random.randint(jax.random.fold_in(key, axis), (), 0, dims[axis]) for axis in range(len(dims))]
    entries = entries.at[tuple(spot)].set(low)
    longest = dims.index(max(dims))
    spot[longest] = (spot[longest] + 1) % dims[longest]
    return entries.at[tuple(spot)].set(largest)


def level_of(stream_key, extent, split, least, largest):
    def one(axis_at, shards_of):
        steps = jax.random.uniform(jax.random.fold_in(jax.random.fold_in(stream_key, 6), axis_at), (shards_of,), jnp.float32, least / len(split), largest / len(split))
        return jnp.repeat(jnp.exp(steps), extent[axis_at] // shards_of).reshape((-1,) + (1,) * (len(extent) - axis_at - 1))

    level = one(*split[0])
    for cut in split[1:]:
        level = level * one(*cut)
    return level


def centred(stream_key, extent, deviation, reach, shards=(), kind=jnp.bfloat16):
    gain = level_of(stream_key, extent, shards, -0.22, 0.18) if shards else 1.0
    array = jax.random.normal(stream_key, extent, jnp.float32) * deviation * gain
    return jnp.minimum(jnp.maximum(array, -reach), reach).astype(kind)


def setup_inputs(seed: int = 0) -> dict:
    seeds = jax.random.split(jax.random.key(seed), 9)
    return {
        "gains": centred(seeds[0], (2, NC, DISHES), 0.8, 5.0, ((1, 32), (2, 16)), jnp.float32),
        "gain_tan": centred(seeds[1], (2, NC, DISHES), 1.0, 6.0, ((1, 32), (2, 16)), jnp.float32),
        "group_vis": centred(seeds[2], (2, NC, GROUPS), 1.0, 6.0, ((1, 32), (2, 16)), jnp.float32),
        "group_tan": centred(seeds[3], (2, NC, GROUPS), 1.0, 6.0, ((1, 32), (2, 16)), jnp.float32),
        "dish_of": jax.random.permutation(seeds[4], DISHES).astype(jnp.int32),
        "group_of": jax.random.permutation(seeds[5], GROUPS).astype(jnp.int32),
        "block_list": draw_block_list(jax.random.fold_in(seeds[8], 71), 0),
        "weights": touch_ends(jax.random.randint(seeds[7], (PAIRS, COLS * COLS), 0, 5), jax.random.fold_in(seeds[7], 1), 0, 4).astype(jnp.int32),
    }


prior_weight = 0.5

def times_complex(left, right):
    return jnp.stack([left[0] * right[0] - left[1] * right[1], left[0] * right[1] + left[1] * right[0]])

def conjugate(values):
    return jnp.stack([values[0], -values[1]])

def reference(gains, gain_tan, group_vis, group_tan, dish_of, group_of, block_list, weights):
    columns = COLS
    offsets = 2 * columns - 1
    chans = gains.shape[1]
    grid_gain = gains[:, :, dish_of].reshape(2, chans, ROWS, columns)
    grid_tan = gain_tan[:, :, dish_of].reshape(2, chans, ROWS, columns)
    front = jnp.zeros((2, chans, columns), jnp.float32)
    grid_vis = jnp.concatenate([front, group_vis[:, :, group_of]], axis=2).reshape(2, chans, ROWS, offsets)
    grid_gtan = jnp.concatenate([front, group_tan[:, :, group_of]], axis=2).reshape(2, chans, ROWS, offsets)
    first_col = jnp.arange(columns)[:, None]
    second_col = jnp.arange(columns)[None, :]
    offset_table = (second_col - first_col + columns - 1).astype(jnp.int32)
    upper = second_col > first_col
    member = (jnp.arange(offsets)[:, None] == offset_table.reshape(-1)[None, :]).astype(jnp.float32)
    norm_factor = 1.0 / jnp.sqrt(jnp.float32(ROWS * columns))

    def one_slot(carry, slot):
        gain_grid, group_grid = carry
        pair_rows, weight_row = slot
        first_row = pair_rows[0]
        second_row = pair_rows[1]
        row_gap = second_row - first_row
        first_gain = grid_gain[:, :, first_row][:, :, :, None]
        second_gain = grid_gain[:, :, second_row][:, :, None, :]
        first_tan = grid_tan[:, :, first_row][:, :, :, None]
        second_tan = grid_tan[:, :, second_row][:, :, None, :]
        vis_row = grid_vis[:, :, row_gap]
        tan_row = grid_gtan[:, :, row_gap]
        toeplitz_vis = vis_row[:, :, offset_table]
        toeplitz_tan = tan_row[:, :, offset_table]
        valid = jnp.where(row_gap == 0, upper, True)
        weight_grid = jnp.where(valid, weight_row.reshape(columns, columns).astype(jnp.float32), 0.0) * norm_factor
        pair_prod = times_complex(first_gain, conjugate(second_gain))
        gain_part = times_complex(first_tan, conjugate(second_gain)) + times_complex(first_gain, conjugate(second_tan))
        model_tan = times_complex(gain_part, toeplitz_vis) + times_complex(pair_prod, toeplitz_tan)
        weighted = model_tan * weight_grid
        first_upd = lax.optimization_barrier(jnp.sum(times_complex(weighted, times_complex(second_gain, conjugate(toeplitz_vis))), axis=3))
        second_upd = lax.optimization_barrier(jnp.sum(times_complex(conjugate(weighted), times_complex(first_gain, toeplitz_vis)), axis=2))
        group_field = times_complex(weighted, conjugate(pair_prod)).reshape(2, chans, columns * columns)
        group_row = jnp.einsum('pcn,jn->pcj', group_field, member, precision=lax.Precision.HIGHEST)
        gain_grid = gain_grid.at[:, :, first_row].add(first_upd)
        gain_grid = gain_grid.at[:, :, second_row].add(second_upd)
        group_grid = group_grid.at[:, :, row_gap].add(group_row)
        return ((gain_grid, group_grid), None)
    start = (jnp.zeros((2, chans, ROWS, columns), jnp.float32), jnp.zeros((2, chans, ROWS, offsets), jnp.float32))
    (gain_grid, group_grid), _ = lax.scan(one_slot, start, (block_list, weights))
    gain_sum = jnp.zeros((2, chans, DISHES), jnp.float32).at[:, :, dish_of].set(gain_grid.reshape(2, chans, DISHES))
    canonical = group_grid.reshape(2, chans, ROWS * offsets)[:, :, columns:]
    group_update = jnp.zeros((2, chans, GROUPS), jnp.float32).at[:, :, group_of].set(canonical)
    padded = jnp.pad(gain_tan, ((0, 0), (1, 1), (0, 0)))
    prior = 2.0 * gain_tan - padded[:, :-2] - padded[:, 2:]
    gain_update = gain_sum + prior_weight * prior
    return (gain_update, group_update)
```

```python
import jax
import jax.numpy as jnp
from jax import lax
from jax.experimental import pallas as pl
from jax.experimental.pallas import tpu as pltpu
from jax.sharding import PartitionSpec as P

ROWS = 32
COLS = 32
DISHES = 1024
GROUPS = 1984
PRIOR_WEIGHT = 0.5

LANES = 128
PEERS = 16
DISH_PART = DISHES // PEERS
GROUP_PART = GROUPS // PEERS
CHANS = 2
SLOTS = 33
SLOT_GROUPS = 5
GATHER_WIDTH = 1536
SCATTER_WIDTH = 768

F32 = jnp.float32
I32 = jnp.int32


def iota(shape, dim):
    return lax.broadcasted_iota(I32, shape, dim)


def by_lane(x, idx):
    return jnp.take_along_axis(x, idx, axis=1)


def by_sublane(x, idx):
    return jnp.take_along_axis(x, idx, axis=0)


def div124(g):
    return ((g >> 2) * 16913) >> 19


def div63(n):
    return (n * 66577) >> 22


def spread(row, rows=8):
    return jnp.broadcast_to(row, (rows, LANES))


def prep_kernel(dish_ref, group_ref, blocks_ref, weights_ref, idx_ref, wts_ref):
    lane = iota((8, LANES), 1)
    sub = iota((8, LANES), 0)
    for half in range(2):
        dy = 16 * half + 2 * sub + (lane >> 6)
        wrapped = lane & 63
        dx = jnp.where(wrapped < 32, wrapped, wrapped - 64)
        k = dy * 63 + dx - 1
        ok = (k >= 0) & (wrapped != 32)
        chunk = k >> 7
        at = k & 127
        first = (16 * half * 63 - 32) // 128
        last = ((16 * half + 15) * 63 + 31) // 128
        found = jnp.zeros((8, LANES), I32)
        for c in range(max(first, 0), min(last, 15) + 1):
            row = spread(group_ref[c : c + 1, :])
            found = jnp.where(chunk == c, by_lane(row, at), found)
        zg = div124(found)
        idx_ref[8 * half : 8 * half + 8, :] = jnp.where(ok, zg, -1)
        idx_ref[16 + 8 * half : 24 + 8 * half, :] = found - 124 * zg
    peer = iota((PEERS, LANES), 0)
    low = iota((LANES, LANES), 0)
    nt = (((1,), (1,)), ((), ()))
    acc = jnp.zeros((2 * PEERS, LANES), F32)
    for c in range(8):
        ids = dish_ref[c : c + 1, :]
        hot = peer == (spread(ids, PEERS) >> 6)
        n_lane = iota((PEERS, LANES), 1)
        left = jnp.concatenate(
            [jnp.where(hot, float(c), 0.0), jnp.where(hot, n_lane, 0).astype(F32)], axis=0
        )
        right = (spread(ids, LANES) & 63) == (low & 63)
        acc = acc + lax.dot_general(
            left.astype(jnp.bfloat16),
            right.astype(F32).astype(jnp.bfloat16),
            nt,
            preferred_element_type=F32,
        )
    idx_ref[32:64, :] = (acc + 0.5).astype(I32)
    acc = jnp.zeros((2 * PEERS, LANES), F32)
    for c in range(16):
        ids = spread(group_ref[c : c + 1, :], PEERS)
        zone = div124(ids)
        n = LANES * c + iota((PEERS, LANES), 1)
        hot = (peer == zone) & (n < GROUPS)
        dy = div63(n + 32)
        dx = n + 32 - 63 * dy - 31
        table_row = dy >> 1
        table_lane = 64 * (dy & 1) + (dx & 63)
        left = jnp.concatenate(
            [jnp.where(hot, table_row, 0), jnp.where(hot, table_lane, 0)], axis=0
        ).astype(F32)
        rest = (ids - 124 * zone)[0:1, :]
        right = spread(rest, LANES) == low
        acc = acc + lax.dot_general(
            left.astype(jnp.bfloat16),
            right.astype(F32).astype(jnp.bfloat16),
            nt,
            preferred_element_type=F32,
        )
    idx_ref[64:96, :] = (acc + 0.5).astype(I32)
    for g in range(SLOT_GROUPS):
        if g < 4:
            pairs = blocks_ref[8 * g : 8 * g + 8, :]
            gap = jnp.broadcast_to(pairs[:, 1:2] - pairs[:, 0:1], (8, LANES))
        else:
            pairs = blocks_ref[32:33, :]
            gap = jnp.broadcast_to(pairs[:, 1:2] - pairs[:, 0:1], (8, LANES))
        for j in range(8):
            cols = slice(LANES * j, LANES * j + LANES)
            first_col = 4 * j + (lane >> 5)
            second_col = lane & 31
            ok = (gap > 0) | (second_col > first_col)
            if g < 4:
                w = weights_ref[8 * g : 8 * g + 8, cols]
            else:
                w = spread(weights_ref[32:33, cols])
                ok = ok & (sub == 0)
            wts_ref[8 * g : 8 * g + 8, cols] = jnp.where(ok, w.astype(F32), 0.0) * (1.0 / 32.0)


def main_kernel(recv_ref, dish_ref, blocks_ref, idx_ref, wts_ref, out_ref, gtab, ytab, ff, ss, gg, gout, yout):
    lane = iota((8, LANES), 1)
    sub = iota((8, LANES), 0)
    quad = lane >> 5
    col = lane & 31
    dish = dish_ref[...]
    zone = dish >> 6
    at = dish & 63
    for b in range(4):
        res = [jnp.zeros((8, LANES), F32), jnp.zeros((8, LANES), F32)]
        for z in range(PEERS):
            row = spread(recv_ref[z, :, LANES * b : LANES * b + LANES])
            hit = zone == z
            for c in range(CHANS):
                res[c] = jnp.where(hit, by_lane(row, at + 64 * c), res[c])
        for c in range(CHANS):
            gtab[2 * b + c] = res[c]
    for b in range(8):
        res = [jnp.zeros((8, LANES), F32), jnp.zeros((8, LANES), F32)]
        for z in range(PEERS):
            row = spread(recv_ref[z, :, 512 + LANES * b : 512 + LANES * b + LANES])
            for h in range(2):
                hit = idx_ref[8 * h : 8 * h + 8, :] == z
                res[h] = jnp.where(hit, by_lane(row, idx_ref[16 + 8 * h : 24 + 8 * h, :]), res[h])
        ytab[b, 0:8, :] = res[0]
        ytab[b, 8:16, :] = res[1]
    half_lo = (lane & 16) == 0
    quarter_lo = (lane & 8) == 0
    eighth_lo = (lane & 4) == 0
    sorted_idx = 32 * (col & 3) + 16 * ((col >> 2) & 1) + 8 * ((col >> 3) & 1) + 4 * ((col >> 4) & 1)

    def merge(a, b, low, bit):
        return jnp.where(low, a, b) + by_lane(jnp.where(low, b, a), lane ^ bit)

    for g in range(SLOT_GROUPS):
        if g < 4:
            pairs = blocks_ref[8 * g : 8 * g + 8, :]
        else:
            pairs = blocks_ref[32:33, :]
        r1 = jnp.broadcast_to(pairs[:, 0:1], (8, LANES))
        r2 = jnp.broadcast_to(pairs[:, 1:2], (8, LANES))
        dy = r2 - r1
        slots = slice(8 * g, 8 * g + 8)
        base1 = 32 * (r1 & 3) + quad
        base2 = 32 * (r2 & 3) + col
        basey = 64 * (dy & 1)
        for c in range(CHANS):
            src_a = [by_sublane(gtab[2 * b + c], r1 >> 2) for b in range(4)]
            gb = [by_lane(by_sublane(gtab[2 * b + c], r2 >> 2), base2) for b in range(4)]
            src_y = []
            for b in range(4):
                low = by_sublane(ytab[2 * b + c, 0:8, :], (dy >> 1) & 7)
                high = by_sublane(ytab[2 * b + c, 8:16, :], (dy >> 1) & 7)
                src_y.append(jnp.where(dy < 16, low, high))
            gbr, gbi, dbr, dbi = gb
            f_re, f_im = [], []
            s_re = s_im = pos_re = pos_im = neg_re = neg_im = None
            for j in range(8):
                idx_a = base1 + 4 * j
                ga_r, ga_i, da_r, da_i = [by_lane(v, idx_a) for v in src_a]
                first_col = 4 * j + quad
                idx_y = basey + ((col - first_col) & 63)
                y_r, y_i, t_r, t_i = [by_lane(v, idx_y) for v in src_y]
                w = wts_ref[slots, LANES * j : LANES * j + LANES]
                p_r = ga_r * gbr + ga_i * gbi
                p_i = ga_i * gbr - ga_r * gbi
                q_r = (da_r * gbr + da_i * gbi) + (ga_r * dbr + ga_i * dbi)
                q_i = (da_i * gbr - da_r * gbi) + (ga_i * dbr - ga_r * dbi)
                u_r = w * ((q_r * y_r - q_i * y_i) + (p_r * t_r - p_i * t_i))
                u_i = w * ((q_r * y_i + q_i * y_r) + (p_r * t_i + p_i * t_r))
                v_r = u_r * y_r + u_i * y_i
                v_i = u_i * y_r - u_r * y_i
                f_re.append(v_r * gbr - v_i * gbi)
                f_im.append(v_r * gbi + v_i * gbr)
                a_r = v_r * ga_r + v_i * ga_i
                a_i = v_r * ga_i - v_i * ga_r
                d_r = u_r * p_r + u_i * p_i
                d_i = u_i * p_r - u_r * p_i
                shift = (lane & 96) | ((col + first_col) & 31)
                straight = col + first_col < 32
                d_r = by_lane(d_r, shift)
                d_i = by_lane(d_i, shift)
                pr = jnp.where(straight, d_r, 0.0)
                pi = jnp.where(straight, d_i, 0.0)
                nr = jnp.where(straight, 0.0, d_r)
                ni = jnp.where(straight, 0.0, d_i)
                if j == 0:
                    s_re, s_im, pos_re, pos_im, neg_re, neg_im = a_r, a_i, pr, pi, nr, ni
                else:
                    s_re = s_re + a_r
                    s_im = s_im + a_i
                    pos_re = pos_re + pr
                    pos_im = pos_im + pi
                    neg_re = neg_re + nr
                    neg_im = neg_im + ni
            here1 = (r1 & 3) == quad
            here2 = (r2 & 3) == quad
            herey = (dy & 1) == (lane >> 6)
            for p, vals in enumerate((f_re, f_im)):
                lv = [merge(vals[2 * k], vals[2 * k + 1], half_lo, 16) for k in range(4)]
                lv = [merge(lv[2 * k], lv[2 * k + 1], quarter_lo, 8) for k in range(2)]
                one = merge(lv[0], lv[1], eighth_lo, 4)
                one = one + by_lane(one, lane ^ 2)
                one = one + by_lane(one, lane ^ 1)
                one = by_lane(one, sorted_idx)
                ff[slots, LANES * (2 * p + c) : LANES * (2 * p + c + 1)] = jnp.where(here1, one, 0.0)
            for p, one in enumerate((s_re, s_im)):
                one = one + by_lane(one, lane ^ 32)
                one = one + by_lane(one, lane ^ 64)
                ff[slice(40 + 8 * g, 48 + 8 * g), LANES * (2 * p + c) : LANES * (2 * p + c + 1)] = jnp.where(
                    here2, one, 0.0
                )
            for p, (a, b) in enumerate(((pos_re, neg_re), (pos_im, neg_im))):
                low = (lane & 32) == 0
                one = merge(a, b, low, 32)
                one = one + by_lane(one, lane ^ 64)
                gg[slots, LANES * (2 * p + c) : LANES * (2 * p + c + 1)] = jnp.where(herey, one, 0.0)
        ss[slots, :] = ((r1 >> 2) == lane).astype(F32)
        ss[slice(40 + 8 * g, 48 + 8 * g), :] = ((r2 >> 2) == lane).astype(F32)
        ss[slice(80 + 8 * g, 88 + 8 * g), :] = ((dy >> 1) == lane).astype(F32)
    tn = (((0,), (0,)), ((), ()))
    gout[...] = lax.dot_general(
        ss[0:80, :], ff[...], tn, precision=lax.Precision.HIGHEST, preferred_element_type=F32
    )[0:8, :]
    yout[...] = lax.dot_general(
        ss[80:120, :], gg[...], tn, precision=lax.Precision.HIGHEST, preferred_element_type=F32
    )[0:16, :]
    for h in range(2):
        rows = slice(8 * h, 8 * h + 8)
        at_row = idx_ref[32 + 8 * h : 40 + 8 * h, :]
        at_lane = idx_ref[48 + 8 * h : 56 + 8 * h, :]
        for p in range(2):
            res = jnp.zeros((8, LANES), F32)
            for c in range(CHANS):
                mine = (lane >> 6) == c
                for k in range(8):
                    row = spread(gout[k : k + 1, LANES * (2 * p + c) : LANES * (2 * p + c + 1)])
                    res = jnp.where(mine & (at_row == k), by_lane(row, at_lane), res)
            out_ref[rows, 0, 512 + LANES * p : 512 + LANES * (p + 1)] = res
        at_row = idx_ref[64 + 8 * h : 72 + 8 * h, :]
        at_lane = idx_ref[80 + 8 * h : 88 + 8 * h, :]
        for q in range(4):
            res = jnp.zeros((8, LANES), F32)
            for k in range(16):
                row = spread(yout[k : k + 1, LANES * q : LANES * (q + 1)])
                res = jnp.where(at_row == k, by_lane(row, at_lane), res)
            out_ref[rows, 0, LANES * q : LANES * (q + 1)] = res


def final_kernel(recv_ref, tan_ref, before_ref, after_ref, gain_ref, group_ref):
    for p in range(2):
        before = before_ref[p]
        after = after_ref[p]
        t0 = tan_ref[p, 0:1, :]
        t1 = tan_ref[p, 1:2, :]
        prior = [2.0 * t0 - before - t1, 2.0 * t1 - t0 - after]
        total = recv_ref[0, :, 512 + LANES * p : 512 + LANES * (p + 1)]
        for z in range(1, PEERS):
            total = total + recv_ref[z, :, 512 + LANES * p : 512 + LANES * (p + 1)]
        for c in range(CHANS):
            gain_ref[p, c : c + 1, :] = total[:, 64 * c : 64 * c + 64] + PRIOR_WEIGHT * prior[c]
            q = 2 * p + c
            sums = recv_ref[0, :, LANES * q : LANES * (q + 1)]
            for z in range(1, PEERS):
                sums = sums + recv_ref[z, :, LANES * q : LANES * (q + 1)]
            group_ref[p, c : c + 1, :] = sums[:, 0:GROUP_PART]


def local(gains, gain_tan, group_vis, group_tan, dish_of, group_of, block_list, weights):
    shape = jax.ShapeDtypeStruct
    pad = ((0, 0), (0, 0), (0, LANES - GROUP_PART))
    message = jnp.concatenate(
        [
            gains.reshape(-1),
            gain_tan.reshape(-1),
            jnp.pad(group_vis, pad).reshape(-1),
            jnp.pad(group_tan, pad).reshape(-1),
        ]
    )
    sent = jnp.broadcast_to(message[None, None], (PEERS, 1, GATHER_WIDTH))
    gathered = lax.all_to_all(sent, "bl", 0, 0, tiled=True)
    peers = lax.axis_size("tf")
    up = [(i, i + 1) for i in range(peers - 1)]
    down = [(j, i) for i, j in up]
    before = lax.ppermute(gain_tan[:, 1:2], "tf", up)
    after = lax.ppermute(gain_tan[:, 0:1], "tf", down)
    dish_table = dish_of.reshape(8, LANES)
    group_table = jnp.pad(group_of, (0, 16 * LANES - GROUPS)).reshape(16, LANES)
    idx, wts = pl.pallas_call(
        prep_kernel,
        out_shape=(shape((96, LANES), I32), shape((8 * SLOT_GROUPS, 1024), F32)),
        name="prep",
    )(dish_table, group_table, block_list, weights)
    partial = pl.pallas_call(
        main_kernel,
        out_shape=shape((PEERS, 1, SCATTER_WIDTH), F32),
        scratch_shapes=[
            pltpu.VMEM((8, 8, LANES), F32),
            pltpu.VMEM((8, 16, LANES), F32),
            pltpu.VMEM((80, 4 * LANES), F32),
            pltpu.VMEM((120, LANES), F32),
            pltpu.VMEM((40, 4 * LANES), F32),
            pltpu.VMEM((8, 4 * LANES), F32),
            pltpu.VMEM((16, 4 * LANES), F32),
        ],
        name="main",
    )(gathered, dish_table, block_list, idx, wts)
    parts = lax.all_to_all(partial, "bl", 0, 0, tiled=True)
    return pl.pallas_call(
        final_kernel,
        out_shape=(shape((2, CHANS, DISH_PART), F32), shape((2, CHANS, GROUP_PART), F32)),
        name="finish",
    )(parts, gain_tan, before, after)


def solution(mesh):
    placed = (
        P(None, "tf", "bl"),
        P(None, "tf", "bl"),
        P(None, "tf", "bl"),
        P(None, "tf", "bl"),
        P(),
        P(),
        P("bl", None),
        P("bl", None),
    )
    return jax.shard_map(
        local,
        mesh=mesh,
        in_specs=placed,
        out_specs=(P(None, "tf", "bl"), P(None, "tf", "bl")),
        check_vma=False,
    )
```

```python
import jax
import jax.numpy as jnp
from jax import lax
from jax.experimental import pallas as pl
from jax.experimental.pallas import tpu as pltpu
from jax.sharding import PartitionSpec as P

ROWS = 32
COLS = 32
DISHES = 1024
GROUPS = 1984
PRIOR_WEIGHT = 0.5

LANES = 128
PEERS = 16
DISH_PART = DISHES // PEERS
GROUP_PART = GROUPS // PEERS
CHANS = 2
SLOTS = 33
SLOT_GROUPS = 5
GATHER_WIDTH = 1536
SCATTER_WIDTH = 768
PARTS = 3

F32 = jnp.float32
I32 = jnp.int32


def iota(shape, dim):
    return lax.broadcasted_iota(I32, shape, dim)


def by_lane(x, idx):
    return jnp.take_along_axis(x, idx, axis=1)


def by_sublane(x, idx):
    return jnp.take_along_axis(x, idx, axis=0)


def div124(g):
    return ((g >> 2) * 16913) >> 19


def div63(n):
    return (n * 66577) >> 22


def spread(row, rows=8):
    return jnp.broadcast_to(row, (rows, LANES))

BF16 = jnp.bfloat16
ROWS_ALL = 8 * 8 * SLOT_GROUPS


def split3(x):
    hi = x.astype(BF16).astype(F32)
    rest = x - hi
    mid = rest.astype(BF16).astype(F32)
    return hi, mid, rest - mid


def pack_kernel(gain_ref, tan_ref, vis_ref, gtan_ref, out_ref):
    for k, ref in enumerate((gain_ref, tan_ref)):
        for p in range(2):
            row = jnp.concatenate([ref[p, 0:1, :], ref[p, 1:2, :]], axis=1)
            at = LANES * (2 * k + p)
            out_ref[:, 0, at : at + LANES] = spread(row, PEERS)
    fill = jnp.zeros((1, LANES - GROUP_PART), F32)
    for k, ref in enumerate((vis_ref, gtan_ref)):
        for p in range(2):
            for c in range(CHANS):
                row = jnp.concatenate([ref[p, c : c + 1, :], fill], axis=1)
                at = 512 + LANES * (4 * k + 2 * p + c)
                out_ref[:, 0, at : at + LANES] = spread(row, PEERS)


def prep_kernel(
    dish_ref, group_ref, blocks_ref, turned_ref, weights_ref,
    idx_ref, wts_ref, hot_ref, e1_ref, e2_ref, ey_ref, s1_ref, sd_ref,
):
    lane = iota((8, LANES), 1)
    sub = iota((8, LANES), 0)
    for half in range(2):
        dy = 16 * half + 2 * sub + (lane >> 6)
        wrapped = lane & 63
        dx = jnp.where(wrapped < 32, wrapped, wrapped - 64)
        k = dy * 63 + dx - 1
        ok = (k >= 0) & (wrapped != 32)
        chunk = k >> 7
        at = k & 127
        first = (16 * half * 63 - 32) // 128
        last = ((16 * half + 15) * 63 + 31) // 128
        found = jnp.zeros((8, LANES), I32)
        for c in range(max(first, 0), min(last, 15) + 1):
            row = spread(group_ref[c : c + 1, :])
            found = jnp.where(chunk == c, by_lane(row, at), found)
        zg = div124(found)
        idx_ref[8 * half : 8 * half + 8, :] = jnp.where(ok, zg, -1)
        idx_ref[16 + 8 * half : 24 + 8 * half, :] = found - 124 * zg
    peer = iota((PEERS, LANES), 0)
    low = iota((LANES, LANES), 0)
    nt = (((1,), (1,)), ((), ()))
    acc = jnp.zeros((2 * PEERS, LANES), F32)
    for c in range(8):
        ids = dish_ref[c : c + 1, :]
        hot = peer == (spread(ids, PEERS) >> 6)
        n_lane = iota((PEERS, LANES), 1)
        left = jnp.concatenate(
            [jnp.where(hot, float(c), 0.0), jnp.where(hot, n_lane, 0).astype(F32)], axis=0
        )
        right = (spread(ids, LANES) & 63) == (low & 63)
        acc = acc + lax.dot_general(
            left.astype(BF16), right.astype(F32).astype(BF16), nt, preferred_element_type=F32
        )
    idx_ref[32:64, :] = (acc + 0.5).astype(I32)
    acc = jnp.zeros((2 * PEERS, LANES), F32)
    for c in range(16):
        ids = spread(group_ref[c : c + 1, :], PEERS)
        zone = div124(ids)
        n = LANES * c + iota((PEERS, LANES), 1)
        hot = (peer == zone) & (n < GROUPS)
        dy = div63(n + 32)
        dx = n + 32 - 63 * dy - 31
        table_row = dy >> 1
        table_lane = 64 * (dy & 1) + (dx & 63)
        left = jnp.concatenate(
            [jnp.where(hot, table_row, 0), jnp.where(hot, table_lane, 0)], axis=0
        ).astype(F32)
        rest = (ids - 124 * zone)[0:1, :]
        right = spread(rest, LANES) == low
        acc = acc + lax.dot_general(
            left.astype(BF16), right.astype(F32).astype(BF16), nt, preferred_element_type=F32
        )
    idx_ref[64:96, :] = (acc + 0.5).astype(I32)
    for g in range(SLOT_GROUPS):
        pairs = blocks_ref[8 * g : 8 * g + 8, :] if g < 4 else blocks_ref[32:33, :]
        gap = jnp.broadcast_to(pairs[:, 1:2] - pairs[:, 0:1], (8, LANES))
        for j in range(8):
            cols = slice(LANES * j, LANES * j + LANES)
            first_col = 4 * j + (lane >> 5)
            second_col = lane & 31
            ok = (gap > 0) | (second_col > first_col)
            if g < 4:
                w = weights_ref[8 * g : 8 * g + 8, cols]
            else:
                w = spread(weights_ref[32:33, cols])
                ok = ok & (sub == 0)
            wts_ref[8 * g : 8 * g + 8, cols] = jnp.where(ok, w.astype(F32), 0.0) * (1.0 / 32.0)
    lane16 = iota((PEERS, LANES), 1)
    one = spread(turned_ref[0:1, :], PEERS)
    two = spread(turned_ref[1:2, :], PEERS)
    ends = jnp.where(lane16 < 40, one, pltpu.roll(two, 40, axis=1))
    hot_ref[0:16, :] = jnp.where((ends >> 2) == peer, 1.0, 0.0).astype(BF16)
    hot_ref[16:32, :] = jnp.where(((two - one) >> 1) == peer, 1.0, 0.0).astype(BF16)
    k = iota((LANES, LANES), 0)
    l = iota((LANES, LANES), 1)
    e2_ref[...] = jnp.where(((k & 31) == (l & 31)) & (k < 96), 1.0, 0.0).astype(BF16)
    for j in range(8):
        cols = slice(LANES * j, LANES * j + LANES)
        c1 = 4 * j + (l >> 5)
        e1_ref[:, cols] = jnp.where(((k & 31) == c1) & (k < 96), 1.0, 0.0).astype(BF16)
        same = (k & 63) == (((l & 31) - c1) & 63)
        ey_ref[0:128, cols] = jnp.where(same, 1.0, 0.0).astype(BF16)
        ey_ref[128:256, cols] = jnp.where(same & (k < 64), 1.0, 0.0).astype(BF16)
        row1 = 4 * j + (k >> 5)
        s1_ref[cols, :] = jnp.where((l & 31) == row1, 1.0, 0.0).astype(BF16)
        sd_ref[cols, :] = jnp.where((l & 63) == (((k & 31) - row1) & 63), 1.0, 0.0).astype(BF16)


def main_kernel(
    recv_ref, dish_ref, blocks_ref, idx_ref, wts_ref, hot_ref, e1_ref, e2_ref, ey_ref, s1_ref, sd_ref,
    tan_ref, before_ref, after_ref,
    out_ref, prior_ref,
    gtab, ytab, la, lb, ly, ga, gb, yy, xf, xd, ff, gg, gout, yout,
):
    lane = iota((8, LANES), 1)
    quad = lane >> 5
    half = lane >> 6
    for p in range(2):
        t0 = tan_ref[p, 0:1, :]
        t1 = tan_ref[p, 1:2, :]
        prior_ref[p, 0:1, :] = PRIOR_WEIGHT * (2.0 * t0 - before_ref[p] - t1)
        prior_ref[p, 1:2, :] = PRIOR_WEIGHT * (2.0 * t1 - t0 - after_ref[p])
    dish = dish_ref[...]
    zone = dish >> 6
    at = dish & 63
    for b in range(4):
        res = [jnp.zeros((8, LANES), F32), jnp.zeros((8, LANES), F32)]
        for z in range(PEERS):
            row = spread(recv_ref[z, :, LANES * b : LANES * b + LANES])
            hit = zone == z
            for c in range(CHANS):
                res[c] = jnp.where(hit, by_lane(row, at + 64 * c), res[c])
        for c in range(CHANS):
            gtab[2 * b + c] = res[c]
    for b in range(8):
        res = [jnp.zeros((8, LANES), F32), jnp.zeros((8, LANES), F32)]
        for z in range(PEERS):
            row = spread(recv_ref[z, :, 512 + LANES * b : 512 + LANES * b + LANES])
            for h in range(2):
                hit = idx_ref[8 * h : 8 * h + 8, :] == z
                res[h] = jnp.where(hit, by_lane(row, idx_ref[16 + 8 * h : 24 + 8 * h, :]), res[h])
        ytab[b, 0:8, :] = res[0]
        ytab[b, 8:16, :] = res[1]
    ends = []
    for g in range(SLOT_GROUPS):
        pairs = blocks_ref[8 * g : 8 * g + 8, :] if g < 4 else blocks_ref[32:33, :]
        r1 = jnp.broadcast_to(pairs[:, 0:1], (8, LANES))
        r2 = jnp.broadcast_to(pairs[:, 1:2], (8, LANES))
        dy = r2 - r1
        ends.append((r1, r2, dy))
        for c in range(CHANS):
            for b in range(4):
                rows = slice(8 * ((2 * g + c) * 4 + b), 8 * ((2 * g + c) * 4 + b) + 8)
                table = gtab[2 * b + c]
                for r, dest in ((r1, la), (r2, lb)):
                    x = jnp.where((r & 3) == quad, by_sublane(table, r >> 2), 0.0)
                    x = x + pltpu.roll(x, 64, axis=1)
                    x = x + pltpu.roll(x, 32, axis=1)
                    hi, mid, lo = split3(x)
                    dest[rows, :] = jnp.where(quad == 0, hi, jnp.where(quad == 1, mid, lo))
                low = by_sublane(ytab[2 * b + c, 0:8, :], (dy >> 1) & 7)
                high = by_sublane(ytab[2 * b + c, 8:16, :], (dy >> 1) & 7)
                x = jnp.where((dy & 1) == half, jnp.where(dy < 16, low, high), 0.0)
                x = x + pltpu.roll(x, 64, axis=1)
                hi, mid, lo = split3(x)
                ly[rows, 0:128] = jnp.where(half == 0, hi, mid)
                ly[rows, 128:256] = lo
    ga[...] = jnp.dot(la[...].astype(BF16), e1_ref[...], preferred_element_type=F32)
    gb[...] = jnp.dot(lb[...].astype(BF16), e2_ref[...], preferred_element_type=F32)
    yy[...] = jnp.dot(ly[...].astype(BF16), ey_ref[...], preferred_element_type=F32)
    for g in range(SLOT_GROUPS):
        r1, r2, dy = ends[g]
        for c in range(CHANS):
            at_rows = [slice(8 * ((2 * g + c) * 4 + b), 8 * ((2 * g + c) * 4 + b) + 8) for b in range(4)]
            gbr, gbi, dbr, dbi = [gb[r, :] for r in at_rows]
            both = slice(16 * (2 * g + c), 16 * (2 * g + c) + 16)
            s_re = s_im = None
            for j in range(8):
                cols = slice(LANES * j, LANES * j + LANES)
                ga_r, ga_i, da_r, da_i = [ga[r, cols] for r in at_rows]
                y_r, y_i, t_r, t_i = [yy[r, cols] for r in at_rows]
                w = wts_ref[8 * g : 8 * g + 8, cols]
                p_r = ga_r * gbr + ga_i * gbi
                p_i = ga_i * gbr - ga_r * gbi
                q_r = (da_r * gbr + da_i * gbi) + (ga_r * dbr + ga_i * dbi)
                q_i = (da_i * gbr - da_r * gbi) + (ga_i * dbr - ga_r * dbi)
                u_r = w * ((q_r * y_r - q_i * y_i) + (p_r * t_r - p_i * t_i))
                u_i = w * ((q_r * y_i + q_i * y_r) + (p_r * t_i + p_i * t_r))
                v_r = u_r * y_r + u_i * y_i
                v_i = u_i * y_r - u_r * y_i
                f = jnp.concatenate([v_r * gbr - v_i * gbi, v_r * gbi + v_i * gbr], axis=0)
                a_r = v_r * ga_r + v_i * ga_i
                a_i = v_r * ga_i - v_i * ga_r
                d = jnp.concatenate([u_r * p_r + u_i * p_i, u_i * p_r - u_r * p_i], axis=0)
                for x, dest in ((f, xf), (d, xd)):
                    for k in range(PARTS):
                        part = x.astype(BF16)
                        dest[k, both, cols] = part
                        if k + 1 < PARTS:
                            x = x - part.astype(F32)
                s_re = a_r if j == 0 else s_re + a_r
                s_im = a_i if j == 0 else s_im + a_i
            for p, one in enumerate((s_re, s_im)):
                one = one + pltpu.roll(one, 64, axis=1)
                one = one + pltpu.roll(one, 32, axis=1)
                dest = slice(LANES * (2 * p + c), LANES * (2 * p + c + 1))
                ff[40 + 8 * g : 48 + 8 * g, dest] = jnp.where((r2 & 3) == quad, one, 0.0)
    first = jnp.dot(xf[0], s1_ref[...], preferred_element_type=F32)
    diag = jnp.dot(xd[0], sd_ref[...], preferred_element_type=F32)
    for k in range(1, PARTS):
        first = first + jnp.dot(xf[k], s1_ref[...], preferred_element_type=F32)
        diag = diag + jnp.dot(xd[k], sd_ref[...], preferred_element_type=F32)
    for g in range(SLOT_GROUPS):
        r1, r2, dy = ends[g]
        for c in range(CHANS):
            for p in range(2):
                rows = slice(16 * (2 * g + c) + 8 * p, 16 * (2 * g + c) + 8 * p + 8)
                dest = slice(LANES * (2 * p + c), LANES * (2 * p + c + 1))
                ff[8 * g : 8 * g + 8, dest] = jnp.where((r1 & 3) == quad, first[rows], 0.0)
                gg[8 * g : 8 * g + 8, dest] = jnp.where((dy & 1) == half, diag[rows], 0.0)
    gsum = ysum = None
    for fx, gx in zip(split3(ff[...]), split3(gg[...])):
        fk = jnp.dot(hot_ref[0:16, 0:80], fx.astype(BF16), preferred_element_type=F32)
        gk = jnp.dot(hot_ref[16:32, 0:40], gx.astype(BF16), preferred_element_type=F32)
        gsum = fk if gsum is None else gsum + fk
        ysum = gk if ysum is None else ysum + gk
    gout[...] = gsum[0:8]
    yout[...] = ysum
    for h in range(2):
        rows = slice(8 * h, 8 * h + 8)
        at_row = idx_ref[32 + 8 * h : 40 + 8 * h, :]
        at_lane = idx_ref[48 + 8 * h : 56 + 8 * h, :]
        for p in range(2):
            res = jnp.zeros((8, LANES), F32)
            for c in range(CHANS):
                mine = half == c
                for k in range(8):
                    row = spread(gout[k : k + 1, LANES * (2 * p + c) : LANES * (2 * p + c + 1)])
                    res = jnp.where(mine & (at_row == k), by_lane(row, at_lane), res)
            out_ref[rows, 0, 512 + LANES * p : 512 + LANES * (p + 1)] = res
        at_row = idx_ref[64 + 8 * h : 72 + 8 * h, :]
        at_lane = idx_ref[80 + 8 * h : 88 + 8 * h, :]
        for q in range(4):
            res = jnp.zeros((8, LANES), F32)
            for k in range(16):
                row = spread(yout[k : k + 1, LANES * q : LANES * (q + 1)])
                res = jnp.where(at_row == k, by_lane(row, at_lane), res)
            out_ref[rows, 0, LANES * q : LANES * (q + 1)] = res


def final_kernel(recv_ref, prior_ref, gain_ref, group_ref):
    for p in range(2):
        at = 512 + LANES * p
        total = recv_ref[0, :, at : at + LANES]
        for z in range(1, PEERS):
            total = total + recv_ref[z, :, at : at + LANES]
        for c in range(CHANS):
            gain_ref[p, c : c + 1, :] = total[:, 64 * c : 64 * c + 64] + prior_ref[p, c : c + 1, :]
            at_q = LANES * (2 * p + c)
            sums = recv_ref[0, :, at_q : at_q + LANES]
            for z in range(1, PEERS):
                sums = sums + recv_ref[z, :, at_q : at_q + LANES]
            group_ref[p, c : c + 1, :] = sums[:, 0:GROUP_PART]


def vmem(count):
    return [pl.BlockSpec(memory_space=pltpu.VMEM)] * count


def local(gains, gain_tan, group_vis, group_tan, dish_of, group_of, block_list, weights):
    shape = jax.ShapeDtypeStruct
    sent = pl.pallas_call(
        pack_kernel,
        in_specs=vmem(4),
        out_specs=vmem(1)[0],
        out_shape=shape((PEERS, 1, GATHER_WIDTH), F32),
        name="pack",
    )(gains, gain_tan, group_vis, group_tan)
    gathered = lax.all_to_all(sent, "bl", 0, 0, tiled=True)
    peers = lax.axis_size("tf")
    up = [(i, i + 1) for i in range(peers - 1)]
    down = [(j, i) for i, j in up]
    before = lax.ppermute(gain_tan[:, 1:2], "tf", up)
    after = lax.ppermute(gain_tan[:, 0:1], "tf", down)
    dish_table = dish_of.reshape(8, LANES)
    group_table = jnp.pad(group_of, (0, 16 * LANES - GROUPS)).reshape(16, LANES)
    turned = jnp.pad(block_list.T, ((0, 0), (0, LANES - SLOTS)))
    tables = pl.pallas_call(
        prep_kernel,
        in_specs=vmem(5),
        out_specs=vmem(8),
        out_shape=(
            shape((96, LANES), I32),
            shape((8 * SLOT_GROUPS, 1024), F32),
            shape((32, LANES), BF16),
            shape((LANES, 1024), BF16),
            shape((LANES, LANES), BF16),
            shape((2 * LANES, 1024), BF16),
            shape((1024, LANES), BF16),
            shape((1024, LANES), BF16),
        ),
        name="prep",
    )(dish_table, group_table, block_list, turned, weights)
    partial, prior = pl.pallas_call(
        main_kernel,
        in_specs=vmem(14),
        out_specs=vmem(2),
        out_shape=(shape((PEERS, 1, SCATTER_WIDTH), F32), shape((2, CHANS, DISH_PART), F32)),
        scratch_shapes=[
            pltpu.VMEM((8, 8, LANES), F32),
            pltpu.VMEM((8, 16, LANES), F32),
            pltpu.VMEM((ROWS_ALL, LANES), F32),
            pltpu.VMEM((ROWS_ALL, LANES), F32),
            pltpu.VMEM((ROWS_ALL, 2 * LANES), F32),
            pltpu.VMEM((ROWS_ALL, 1024), F32),
            pltpu.VMEM((ROWS_ALL, LANES), F32),
            pltpu.VMEM((ROWS_ALL, 1024), F32),
            pltpu.VMEM((PARTS, ROWS_ALL // 2, 1024), BF16),
            pltpu.VMEM((PARTS, ROWS_ALL // 2, 1024), BF16),
            pltpu.VMEM((80, 4 * LANES), F32),
            pltpu.VMEM((40, 4 * LANES), F32),
            pltpu.VMEM((8, 4 * LANES), F32),
            pltpu.VMEM((16, 4 * LANES), F32),
        ],
        name="main",
    )(gathered, dish_table, block_list, *tables, gain_tan, before, after)
    parts = lax.all_to_all(partial, "bl", 0, 0, tiled=True)
    return pl.pallas_call(
        final_kernel,
        in_specs=vmem(2),
        out_specs=vmem(2),
        out_shape=(shape((2, CHANS, DISH_PART), F32), shape((2, CHANS, GROUP_PART), F32)),
        name="finish",
    )(parts, prior)


def solution(mesh):
    placed = (
        P(None, "tf", "bl"),
        P(None, "tf", "bl"),
        P(None, "tf", "bl"),
        P(None, "tf", "bl"),
        P(),
        P(),
        P("bl", None),
        P("bl", None),
    )
    return jax.shard_map(
        local,
        mesh=mesh,
        in_specs=placed,
        out_specs=(P(None, "tf", "bl"), P(None, "tf", "bl")),
        check_vma=False,
    )
```

```python
import jax
import jax.numpy as jnp
from jax import lax
from jax.experimental import pallas as pl
from jax.experimental.pallas import tpu as pltpu
from jax.sharding import PartitionSpec as P

ROWS = 32
COLS = 32
DISHES = 1024
GROUPS = 1984
PRIOR_WEIGHT = 0.5

LANES = 128
PEERS = 16
DISH_PART = DISHES // PEERS
GROUP_PART = GROUPS // PEERS
CHANS = 2
SLOTS = 33
SLOT_GROUPS = 5
GATHER_WIDTH = 1536
SCATTER_WIDTH = 768
PARTS = 2

F32 = jnp.float32
I32 = jnp.int32


def iota(shape, dim):
    return lax.broadcasted_iota(I32, shape, dim)


def by_lane(x, idx):
    return jnp.take_along_axis(x, idx, axis=1)


def by_sublane(x, idx):
    return jnp.take_along_axis(x, idx, axis=0)


def div124(g):
    return ((g >> 2) * 16913) >> 19


def div63(n):
    return (n * 66577) >> 22


def spread(row, rows=8):
    return jnp.broadcast_to(row, (rows, LANES))

BF16 = jnp.bfloat16
ROWS_ALL = 8 * 8 * SLOT_GROUPS


def split3(x):
    hi = x.astype(BF16).astype(F32)
    rest = x - hi
    mid = rest.astype(BF16).astype(F32)
    return hi, mid, rest - mid


def pack_kernel(gain_ref, tan_ref, vis_ref, gtan_ref, out_ref):
    for k, ref in enumerate((gain_ref, tan_ref)):
        for p in range(2):
            row = jnp.concatenate([ref[p, 0:1, :], ref[p, 1:2, :]], axis=1)
            at = LANES * (2 * k + p)
            out_ref[:, 0, at : at + LANES] = spread(row, PEERS)
    fill = jnp.zeros((1, LANES - GROUP_PART), F32)
    for k, ref in enumerate((vis_ref, gtan_ref)):
        for p in range(2):
            for c in range(CHANS):
                row = jnp.concatenate([ref[p, c : c + 1, :], fill], axis=1)
                at = 512 + LANES * (4 * k + 2 * p + c)
                out_ref[:, 0, at : at + LANES] = spread(row, PEERS)


def prep_kernel(
    dish_ref, group_ref, blocks_ref, turned_ref, weights_ref,
    idx_ref, ends_ref, wts_ref, hot_ref, e1_ref, e2_ref, ey_ref, s1_ref, sd_ref,
):
    lane = iota((8, LANES), 1)
    sub = iota((8, LANES), 0)
    for half in range(2):
        dy = 16 * half + 2 * sub + (lane >> 6)
        wrapped = lane & 63
        dx = jnp.where(wrapped < 32, wrapped, wrapped - 64)
        k = dy * 63 + dx - 1
        ok = (k >= 0) & (wrapped != 32)
        chunk = k >> 7
        at = k & 127
        first = (16 * half * 63 - 32) // 128
        last = ((16 * half + 15) * 63 + 31) // 128
        found = jnp.zeros((8, LANES), I32)
        for c in range(max(first, 0), min(last, 15) + 1):
            row = spread(group_ref[c : c + 1, :])
            found = jnp.where(chunk == c, by_lane(row, at), found)
        zg = div124(found)
        idx_ref[8 * half : 8 * half + 8, :] = jnp.where(ok, zg, -1)
        idx_ref[16 + 8 * half : 24 + 8 * half, :] = found - 124 * zg
    peer = iota((PEERS, LANES), 0)
    low = iota((LANES, LANES), 0)
    nt = (((1,), (1,)), ((), ()))
    acc = jnp.zeros((PEERS, LANES), F32)
    for c in range(8):
        ids = spread(dish_ref[c : c + 1, :])
        hot = sub == ((ids >> 6) & 7)
        left = jnp.concatenate(
            [jnp.where(hot, float(c), 0.0), jnp.where(hot, lane, 0).astype(F32)], axis=0
        )
        right = spread((ids & 63)[0:1] + 64 * (ids >> 9)[0:1], LANES) == low
        acc = acc + lax.dot_general(
            left.astype(BF16), right.astype(F32).astype(BF16), nt, preferred_element_type=F32
        )
    idx_ref[32:48, :] = (acc + 0.5).astype(I32)
    dish = dish_ref[...]
    idx_ref[80:88, :] = (dish >> 6) & 7
    idx_ref[88:96, :] = (dish & 63) + 64 * (dish >> 9)
    acc = jnp.zeros((2 * PEERS, LANES), F32)
    for c in range(16):
        ids = spread(group_ref[c : c + 1, :], PEERS)
        zone = div124(ids)
        n = LANES * c + iota((PEERS, LANES), 1)
        hot = (peer == zone) & (n < GROUPS)
        dy = div63(n + 32)
        dx = n + 32 - 63 * dy - 31
        table_row = dy >> 1
        table_lane = 64 * (dy & 1) + (dx & 63)
        left = jnp.concatenate(
            [jnp.where(hot, table_row, 0), jnp.where(hot, table_lane, 0)], axis=0
        ).astype(F32)
        rest = (ids - 124 * zone)[0:1, :]
        right = spread(rest, LANES) == low
        acc = acc + lax.dot_general(
            left.astype(BF16), right.astype(F32).astype(BF16), nt, preferred_element_type=F32
        )
    idx_ref[48:80, :] = (acc + 0.5).astype(I32)
    for g in range(SLOT_GROUPS):
        pairs = blocks_ref[8 * g : 8 * g + 8, :] if g < 4 else blocks_ref[32:33, :]
        one = jnp.broadcast_to(pairs[:, 0:1], (8, LANES))
        two = jnp.broadcast_to(pairs[:, 1:2], (8, LANES))
        gap = two - one
        ends_ref[8 * g : 8 * g + 8, :] = one
        ends_ref[40 + 8 * g : 48 + 8 * g, :] = two
        ends_ref[80 + 8 * g : 88 + 8 * g, :] = gap
        for j in range(8):
            cols = slice(LANES * j, LANES * j + LANES)
            first_col = 4 * j + (lane >> 5)
            second_col = lane & 31
            ok = (gap > 0) | (second_col > first_col)
            if g < 4:
                w = weights_ref[8 * g : 8 * g + 8, cols]
            else:
                w = spread(weights_ref[32:33, cols])
                ok = ok & (sub == 0)
            wts_ref[8 * g : 8 * g + 8, cols] = jnp.where(ok, w.astype(F32), 0.0) * (1.0 / 32.0)
    lane16 = iota((PEERS, LANES), 1)
    one = spread(turned_ref[0:1, :], PEERS)
    two = spread(turned_ref[1:2, :], PEERS)
    ends = jnp.where(lane16 < 40, one, pltpu.roll(two, 40, axis=1))
    hot_ref[0:16, :] = jnp.where((ends >> 2) == peer, 1.0, 0.0).astype(BF16)
    hot_ref[16:32, :] = jnp.where(((two - one) >> 1) == peer, 1.0, 0.0).astype(BF16)
    k = iota((LANES, LANES), 0)
    l = iota((LANES, LANES), 1)
    e2_ref[...] = jnp.where(((k & 31) == (l & 31)) & (k < 96), 1.0, 0.0).astype(BF16)
    for j in range(8):
        cols = slice(LANES * j, LANES * j + LANES)
        c1 = 4 * j + (l >> 5)
        e1_ref[:, cols] = jnp.where(((k & 31) == c1) & (k < 96), 1.0, 0.0).astype(BF16)
        same = (k & 63) == (((l & 31) - c1) & 63)
        ey_ref[0:128, cols] = jnp.where(same, 1.0, 0.0).astype(BF16)
        ey_ref[128:256, cols] = jnp.where(same & (k < 64), 1.0, 0.0).astype(BF16)
        row1 = 4 * j + (k >> 5)
        s1_ref[cols, :] = jnp.where((l & 31) == row1, 1.0, 0.0).astype(BF16)
        sd_ref[cols, :] = jnp.where((l & 63) == (((k & 31) - row1) & 63), 1.0, 0.0).astype(BF16)


def main_kernel(
    recv_ref, idx_ref, ends_ref, wts_ref, hot_ref, e1_ref, e2_ref, ey_ref, s1_ref, sd_ref,
    out_ref,
    gsrc, gtab, ytab, la, lb, ly, ga, gb, yy, xf, xd, ff, gg, gout, yout,
):
    lane = iota((8, LANES), 1)
    quad = lane >> 5
    half = lane >> 6
    at_row = idx_ref[80:88, :]
    at_lane = idx_ref[88:96, :]
    left = half == 0
    for b in range(4):
        one = recv_ref[0:8, 0, LANES * b : LANES * b + LANES]
        two = recv_ref[8:16, 0, LANES * b : LANES * b + LANES]
        gsrc[2 * b] = jnp.where(left, one, pltpu.roll(two, 64, axis=1))
        gsrc[2 * b + 1] = jnp.where(left, pltpu.roll(one, 64, axis=1), two)
    for q in range(8):
        res = by_lane(spread(gsrc[q, 0:1, :]), at_lane)
        for k in range(1, 8):
            res = jnp.where(at_row == k, by_lane(spread(gsrc[q, k : k + 1, :]), at_lane), res)
        gtab[q] = res
    for b in range(8):
        res = [jnp.zeros((8, LANES), F32), jnp.zeros((8, LANES), F32)]
        for z in range(PEERS):
            row = spread(recv_ref[z, :, 512 + LANES * b : 512 + LANES * b + LANES])
            for h in range(2):
                hit = idx_ref[8 * h : 8 * h + 8, :] == z
                res[h] = jnp.where(hit, by_lane(row, idx_ref[16 + 8 * h : 24 + 8 * h, :]), res[h])
        ytab[b, 0:8, :] = res[0]
        ytab[b, 8:16, :] = res[1]
    ends = []
    for g in range(SLOT_GROUPS):
        r1 = ends_ref[8 * g : 8 * g + 8, :]
        r2 = ends_ref[40 + 8 * g : 48 + 8 * g, :]
        dy = ends_ref[80 + 8 * g : 88 + 8 * g, :]
        ends.append((r1, r2, dy))
        for c in range(CHANS):
            for b in range(4):
                rows = slice(8 * ((2 * g + c) * 4 + b), 8 * ((2 * g + c) * 4 + b) + 8)
                table = gtab[2 * b + c]
                for r, dest in ((r1, la), (r2, lb)):
                    x = jnp.where((r & 3) == quad, by_sublane(table, r >> 2), 0.0)
                    x = x + pltpu.roll(x, 64, axis=1)
                    x = x + pltpu.roll(x, 32, axis=1)
                    hi, mid, lo = split3(x)
                    dest[rows, :] = jnp.where(quad == 0, hi, jnp.where(quad == 1, mid, lo))
                low = by_sublane(ytab[2 * b + c, 0:8, :], (dy >> 1) & 7)
                high = by_sublane(ytab[2 * b + c, 8:16, :], (dy >> 1) & 7)
                x = jnp.where((dy & 1) == half, jnp.where(dy < 16, low, high), 0.0)
                x = x + pltpu.roll(x, 64, axis=1)
                hi, mid, lo = split3(x)
                ly[rows, 0:128] = jnp.where(half == 0, hi, mid)
                ly[rows, 128:256] = lo
    ga[...] = jnp.dot(la[...].astype(BF16), e1_ref[...], preferred_element_type=F32)
    gb[...] = jnp.dot(lb[...].astype(BF16), e2_ref[...], preferred_element_type=F32)
    yy[...] = jnp.dot(ly[...].astype(BF16), ey_ref[...], preferred_element_type=F32)
    for g in range(SLOT_GROUPS):
        r1, r2, dy = ends[g]
        for c in range(CHANS):
            at_rows = [slice(8 * ((2 * g + c) * 4 + b), 8 * ((2 * g + c) * 4 + b) + 8) for b in range(4)]
            gbr, gbi, dbr, dbi = [gb[r, :] for r in at_rows]
            both = slice(16 * (2 * g + c), 16 * (2 * g + c) + 16)
            s_re = s_im = None
            for j in range(8):
                cols = slice(LANES * j, LANES * j + LANES)
                ga_r, ga_i, da_r, da_i = [ga[r, cols] for r in at_rows]
                y_r, y_i, t_r, t_i = [yy[r, cols] for r in at_rows]
                w = wts_ref[8 * g : 8 * g + 8, cols]
                p_r = ga_r * gbr + ga_i * gbi
                p_i = ga_i * gbr - ga_r * gbi
                q_r = (da_r * gbr + da_i * gbi) + (ga_r * dbr + ga_i * dbi)
                q_i = (da_i * gbr - da_r * gbi) + (ga_i * dbr - ga_r * dbi)
                u_r = w * ((q_r * y_r - q_i * y_i) + (p_r * t_r - p_i * t_i))
                u_i = w * ((q_r * y_i + q_i * y_r) + (p_r * t_i + p_i * t_r))
                v_r = u_r * y_r + u_i * y_i
                v_i = u_i * y_r - u_r * y_i
                f = jnp.concatenate([v_r * gbr - v_i * gbi, v_r * gbi + v_i * gbr], axis=0)
                a_r = v_r * ga_r + v_i * ga_i
                a_i = v_r * ga_i - v_i * ga_r
                d = jnp.concatenate([u_r * p_r + u_i * p_i, u_i * p_r - u_r * p_i], axis=0)
                for x, dest in ((f, xf), (d, xd)):
                    for k in range(PARTS):
                        part = x.astype(BF16)
                        dest[k, both, cols] = part
                        if k + 1 < PARTS:
                            x = x - part.astype(F32)
                s_re = a_r if j == 0 else s_re + a_r
                s_im = a_i if j == 0 else s_im + a_i
            for p, one in enumerate((s_re, s_im)):
                one = one + pltpu.roll(one, 64, axis=1)
                one = one + pltpu.roll(one, 32, axis=1)
                dest = slice(LANES * (2 * p + c), LANES * (2 * p + c + 1))
                ff[40 + 8 * g : 48 + 8 * g, dest] = jnp.where((r2 & 3) == quad, one, 0.0)
    first = jnp.dot(xf[0], s1_ref[...], preferred_element_type=F32)
    diag = jnp.dot(xd[0], sd_ref[...], preferred_element_type=F32)
    for k in range(1, PARTS):
        first = first + jnp.dot(xf[k], s1_ref[...], preferred_element_type=F32)
        diag = diag + jnp.dot(xd[k], sd_ref[...], preferred_element_type=F32)
    for g in range(SLOT_GROUPS):
        r1, r2, dy = ends[g]
        for c in range(CHANS):
            for p in range(2):
                rows = slice(16 * (2 * g + c) + 8 * p, 16 * (2 * g + c) + 8 * p + 8)
                dest = slice(LANES * (2 * p + c), LANES * (2 * p + c + 1))
                ff[8 * g : 8 * g + 8, dest] = jnp.where((r1 & 3) == quad, first[rows], 0.0)
                gg[8 * g : 8 * g + 8, dest] = jnp.where((dy & 1) == half, diag[rows], 0.0)
    gsum = ysum = None
    for fx, gx in zip(split3(ff[...]), split3(gg[...])):
        fk = jnp.dot(hot_ref[0:16, 0:80], fx.astype(BF16), preferred_element_type=F32)
        gk = jnp.dot(hot_ref[16:32, 0:40], gx.astype(BF16), preferred_element_type=F32)
        gsum = fk if gsum is None else gsum + fk
        ysum = gk if ysum is None else ysum + gk
    gout[...] = gsum[0:8]
    yout[...] = ysum
    at_row = idx_ref[32:40, :]
    at_lane = idx_ref[40:48, :]
    for p in range(2):
        res = []
        for c in range(CHANS):
            cols = slice(LANES * (2 * p + c), LANES * (2 * p + c + 1))
            one = by_lane(spread(gout[0:1, cols]), at_lane)
            for k in range(1, 8):
                one = jnp.where(at_row == k, by_lane(spread(gout[k : k + 1, cols]), at_lane), one)
            res.append(one)
        dest = slice(512 + LANES * p, 512 + LANES * (p + 1))
        out_ref[0:8, 0, dest] = jnp.where(left, res[0], pltpu.roll(res[1], 64, axis=1))
        out_ref[8:16, 0, dest] = jnp.where(left, pltpu.roll(res[0], 64, axis=1), res[1])
    for h in range(2):
        at_row = idx_ref[48 + 8 * h : 56 + 8 * h, :]
        at_lane = idx_ref[64 + 8 * h : 72 + 8 * h, :]
        for q in range(4):
            cols = slice(LANES * q, LANES * (q + 1))
            res = by_lane(spread(yout[0:1, cols]), at_lane)
            for k in range(1, 16):
                res = jnp.where(at_row == k, by_lane(spread(yout[k : k + 1, cols]), at_lane), res)
            out_ref[8 * h : 8 * h + 8, 0, cols] = res


def final_kernel(recv_ref, tan_ref, before_ref, after_ref, gain_ref, group_ref):
    for p in range(2):
        t0 = tan_ref[p, 0:1, :]
        t1 = tan_ref[p, 1:2, :]
        prior = [2.0 * t0 - before_ref[p] - t1, 2.0 * t1 - t0 - after_ref[p]]
        at = 512 + LANES * p
        total = recv_ref[0, :, at : at + LANES]
        for z in range(1, PEERS):
            total = total + recv_ref[z, :, at : at + LANES]
        for c in range(CHANS):
            gain_ref[p, c : c + 1, :] = total[:, 64 * c : 64 * c + 64] + PRIOR_WEIGHT * prior[c]
            at_q = LANES * (2 * p + c)
            sums = recv_ref[0, :, at_q : at_q + LANES]
            for z in range(1, PEERS):
                sums = sums + recv_ref[z, :, at_q : at_q + LANES]
            group_ref[p, c : c + 1, :] = sums[:, 0:GROUP_PART]


def near(x):
    return pltpu.with_memory_space_constraint(x, pltpu.VMEM)


def vmem(count):
    return [pl.BlockSpec(memory_space=pltpu.VMEM)] * count


def local(gains, gain_tan, group_vis, group_tan, dish_of, group_of, block_list, weights):
    shape = jax.ShapeDtypeStruct
    sent = pl.pallas_call(
        pack_kernel,
        in_specs=vmem(4),
        out_specs=vmem(1)[0],
        out_shape=pltpu.VMEM((PEERS, 1, GATHER_WIDTH), F32),
        name="pack",
    )(gains, gain_tan, group_vis, group_tan)
    gathered = lax.all_to_all(sent, "bl", 0, 0, tiled=True)
    peers = lax.axis_size("tf")
    up = [(i, i + 1) for i in range(peers - 1)]
    down = [(j, i) for i, j in up]
    before = lax.ppermute(gain_tan[:, 1:2], "tf", up)
    after = lax.ppermute(gain_tan[:, 0:1], "tf", down)
    dish_table = dish_of.reshape(8, LANES)
    group_table = jnp.pad(group_of, (0, 16 * LANES - GROUPS)).reshape(16, LANES)
    turned = jnp.pad(block_list.T, ((0, 0), (0, LANES - SLOTS)))
    tables = pl.pallas_call(
        prep_kernel,
        in_specs=vmem(5),
        out_specs=vmem(9),
        out_shape=(
            pltpu.VMEM((96, LANES), I32),
            pltpu.VMEM((120, LANES), I32),
            pltpu.VMEM((8 * SLOT_GROUPS, 1024), F32),
            pltpu.VMEM((32, LANES), BF16),
            pltpu.VMEM((LANES, 1024), BF16),
            pltpu.VMEM((LANES, LANES), BF16),
            pltpu.VMEM((2 * LANES, 1024), BF16),
            pltpu.VMEM((1024, LANES), BF16),
            pltpu.VMEM((1024, LANES), BF16),
        ),
        name="prep",
    )(dish_table, group_table, block_list, turned, weights)
    partial = pl.pallas_call(
        main_kernel,
        in_specs=vmem(10),
        out_specs=vmem(1)[0],
        out_shape=pltpu.VMEM((PEERS, 1, SCATTER_WIDTH), F32),
        scratch_shapes=[
            pltpu.VMEM((8, 8, LANES), F32),
            pltpu.VMEM((8, 8, LANES), F32),
            pltpu.VMEM((8, 16, LANES), F32),
            pltpu.VMEM((ROWS_ALL, LANES), F32),
            pltpu.VMEM((ROWS_ALL, LANES), F32),
            pltpu.VMEM((ROWS_ALL, 2 * LANES), F32),
            pltpu.VMEM((ROWS_ALL, 1024), F32),
            pltpu.VMEM((ROWS_ALL, LANES), F32),
            pltpu.VMEM((ROWS_ALL, 1024), F32),
            pltpu.VMEM((PARTS, ROWS_ALL // 2, 1024), BF16),
            pltpu.VMEM((PARTS, ROWS_ALL // 2, 1024), BF16),
            pltpu.VMEM((80, 4 * LANES), F32),
            pltpu.VMEM((40, 4 * LANES), F32),
            pltpu.VMEM((8, 4 * LANES), F32),
            pltpu.VMEM((16, 4 * LANES), F32),
        ],
        name="main",
    )(near(gathered), *[near(a) for a in tables])
    parts = lax.all_to_all(partial, "bl", 0, 0, tiled=True)
    return pl.pallas_call(
        final_kernel,
        in_specs=vmem(4),
        out_specs=vmem(2),
        out_shape=(shape((2, CHANS, DISH_PART), F32), shape((2, CHANS, GROUP_PART), F32)),
        name="finish",
    )(near(parts), near(gain_tan), near(before), near(after))


def solution(mesh):
    placed = (
        P(None, "tf", "bl"),
        P(None, "tf", "bl"),
        P(None, "tf", "bl"),
        P(None, "tf", "bl"),
        P(),
        P(),
        P("bl", None),
        P("bl", None),
    )
    return jax.shard_map(
        local,
        mesh=mesh,
        in_specs=placed,
        out_specs=(P(None, "tf", "bl"), P(None, "tf", "bl")),
        check_vma=False,
    )
```

```python
import jax
import jax.numpy as jnp
from jax import lax
from jax.experimental import pallas as pl
from jax.experimental.pallas import tpu as pltpu
from jax.sharding import PartitionSpec as P

ROWS = 32
COLS = 32
DISHES = 1024
GROUPS = 1984
PRIOR_WEIGHT = 0.5

LANES = 128
PEERS = 16
DISH_PART = DISHES // PEERS
GROUP_PART = GROUPS // PEERS
CHANS = 2
SLOTS = 33
SLOT_GROUPS = 5
GATHER_WIDTH = 1536
SCATTER_WIDTH = 768
PARTS = 2
LEAD = 12
STEP = 1
UNSTEP = 1

F32 = jnp.float32
I32 = jnp.int32


def iota(shape, dim):
    return lax.broadcasted_iota(I32, shape, dim)


def by_lane(x, idx):
    return jnp.take_along_axis(x, idx, axis=1)


def by_sublane(x, idx):
    return jnp.take_along_axis(x, idx, axis=0)


def div124(g):
    return ((g >> 2) * 16913) >> 19


def div63(n):
    return (n * 66577) >> 22


def place(z):
    return ((z - LEAD) * UNSTEP) & (PEERS - 1)


def spread(row, rows=8):
    return jnp.broadcast_to(row, (rows, LANES))

BF16 = jnp.bfloat16
ROWS_ALL = 8 * 8 * SLOT_GROUPS


def split3(x):
    hi = x.astype(BF16).astype(F32)
    rest = x - hi
    mid = rest.astype(BF16).astype(F32)
    return hi, mid, rest - mid


def pack_kernel(gain_ref, tan_ref, vis_ref, gtan_ref, out_ref):
    for k, ref in enumerate((gain_ref, tan_ref)):
        for p in range(2):
            row = jnp.concatenate([ref[p, 0:1, :], ref[p, 1:2, :]], axis=1)
            at = LANES * (2 * k + p)
            out_ref[:, 0, at : at + LANES] = spread(row, PEERS)
    fill = jnp.zeros((1, LANES - GROUP_PART), F32)
    for k, ref in enumerate((vis_ref, gtan_ref)):
        for p in range(2):
            for c in range(CHANS):
                row = jnp.concatenate([ref[p, c : c + 1, :], fill], axis=1)
                at = 512 + LANES * (4 * k + 2 * p + c)
                out_ref[:, 0, at : at + LANES] = spread(row, PEERS)


def prep_kernel(
    dish_ref, group_ref, blocks_ref, turned_ref, weights_ref,
    idx_ref, ends_ref, wts_ref, hot_ref, e1_ref, e2_ref, ey_ref, s1_ref, sd_ref,
):
    lane = iota((8, LANES), 1)
    sub = iota((8, LANES), 0)
    for half in range(2):
        dy = 16 * half + 2 * sub + (lane >> 6)
        wrapped = lane & 63
        dx = jnp.where(wrapped < 32, wrapped, wrapped - 64)
        k = dy * 63 + dx - 1
        ok = (k >= 0) & (wrapped != 32)
        chunk = k >> 7
        at = k & 127
        first = (16 * half * 63 - 32) // 128
        last = ((16 * half + 15) * 63 + 31) // 128
        found = jnp.zeros((8, LANES), I32)
        for c in range(max(first, 0), min(last, 15) + 1):
            row = spread(group_ref[c : c + 1, :])
            found = jnp.where(chunk == c, by_lane(row, at), found)
        zg = div124(found)
        idx_ref[8 * half : 8 * half + 8, :] = jnp.where(ok, place(zg), -1)
        idx_ref[16 + 8 * half : 24 + 8 * half, :] = found - 124 * zg
    peer = iota((PEERS, LANES), 0)
    low = iota((LANES, LANES), 0)
    nt = (((1,), (1,)), ((), ()))
    acc = jnp.zeros((PEERS, LANES), F32)
    for c in range(8):
        ids = spread(dish_ref[c : c + 1, :])
        zone = place(ids >> 6)
        hot = sub == (zone & 7)
        left = jnp.concatenate(
            [jnp.where(hot, float(c), 0.0), jnp.where(hot, lane, 0).astype(F32)], axis=0
        )
        right = spread((ids & 63)[0:1] + 64 * (zone >> 3)[0:1], LANES) == low
        acc = acc + lax.dot_general(
            left.astype(BF16), right.astype(F32).astype(BF16), nt, preferred_element_type=F32
        )
    idx_ref[32:48, :] = (acc + 0.5).astype(I32)
    dish = dish_ref[...]
    zone = place(dish >> 6)
    idx_ref[80:88, :] = zone & 7
    idx_ref[88:96, :] = (dish & 63) + 64 * (zone >> 3)
    acc = jnp.zeros((2 * PEERS, LANES), F32)
    for c in range(16):
        ids = spread(group_ref[c : c + 1, :], PEERS)
        zone = div124(ids)
        n = LANES * c + iota((PEERS, LANES), 1)
        hot = (peer == place(zone)) & (n < GROUPS)
        dy = div63(n + 32)
        dx = n + 32 - 63 * dy - 31
        table_row = dy >> 1
        table_lane = 64 * (dy & 1) + (dx & 63)
        left = jnp.concatenate(
            [jnp.where(hot, table_row, 0), jnp.where(hot, table_lane, 0)], axis=0
        ).astype(F32)
        rest = (ids - 124 * zone)[0:1, :]
        right = spread(rest, LANES) == low
        acc = acc + lax.dot_general(
            left.astype(BF16), right.astype(F32).astype(BF16), nt, preferred_element_type=F32
        )
    idx_ref[48:80, :] = (acc + 0.5).astype(I32)
    for g in range(SLOT_GROUPS):
        pairs = blocks_ref[8 * g : 8 * g + 8, :] if g < 4 else blocks_ref[32:33, :]
        one = jnp.broadcast_to(pairs[:, 0:1], (8, LANES))
        two = jnp.broadcast_to(pairs[:, 1:2], (8, LANES))
        gap = two - one
        ends_ref[8 * g : 8 * g + 8, :] = one
        ends_ref[40 + 8 * g : 48 + 8 * g, :] = two
        ends_ref[80 + 8 * g : 88 + 8 * g, :] = gap
        for j in range(8):
            cols = slice(LANES * j, LANES * j + LANES)
            first_col = 4 * j + (lane >> 5)
            second_col = lane & 31
            ok = (gap > 0) | (second_col > first_col)
            if g < 4:
                w = weights_ref[8 * g : 8 * g + 8, cols]
            else:
                w = spread(weights_ref[32:33, cols])
                ok = ok & (sub == 0)
            wts_ref[8 * g : 8 * g + 8, cols] = jnp.where(ok, w.astype(F32), 0.0) * (1.0 / 32.0)
    lane16 = iota((PEERS, LANES), 1)
    one = spread(turned_ref[0:1, :], PEERS)
    two = spread(turned_ref[1:2, :], PEERS)
    ends = jnp.where(lane16 < 40, one, pltpu.roll(two, 40, axis=1))
    hot_ref[0:16, :] = jnp.where((ends >> 2) == peer, 1.0, 0.0).astype(BF16)
    hot_ref[16:32, :] = jnp.where(((two - one) >> 1) == peer, 1.0, 0.0).astype(BF16)
    k = iota((LANES, LANES), 0)
    l = iota((LANES, LANES), 1)
    e2_ref[...] = jnp.where(((k & 31) == (l & 31)) & (k < 96), 1.0, 0.0).astype(BF16)
    for j in range(8):
        cols = slice(LANES * j, LANES * j + LANES)
        c1 = 4 * j + (l >> 5)
        e1_ref[:, cols] = jnp.where(((k & 31) == c1) & (k < 96), 1.0, 0.0).astype(BF16)
        same = (k & 63) == (((l & 31) - c1) & 63)
        ey_ref[0:128, cols] = jnp.where(same, 1.0, 0.0).astype(BF16)
        ey_ref[128:256, cols] = jnp.where(same & (k < 64), 1.0, 0.0).astype(BF16)
        row1 = 4 * j + (k >> 5)
        s1_ref[cols, :] = jnp.where((l & 31) == row1, 1.0, 0.0).astype(BF16)
        sd_ref[cols, :] = jnp.where((l & 63) == (((k & 31) - row1) & 63), 1.0, 0.0).astype(BF16)


def main_kernel(
    recv_ref, idx_ref, ends_ref, wts_ref, hot_ref, e1_ref, e2_ref, ey_ref, s1_ref, sd_ref,
    out_ref,
    gsrc, gtab, ytab, la, lb, ly, ga, gb, yy, xf, xd, ff, gg, gout, yout,
):
    lane = iota((8, LANES), 1)
    quad = lane >> 5
    half = lane >> 6
    at_row = idx_ref[80:88, :]
    at_lane = idx_ref[88:96, :]
    left = half == 0
    for b in range(4):
        one = recv_ref[0:8, 0, LANES * b : LANES * b + LANES]
        two = recv_ref[8:16, 0, LANES * b : LANES * b + LANES]
        gsrc[2 * b] = jnp.where(left, one, pltpu.roll(two, 64, axis=1))
        gsrc[2 * b + 1] = jnp.where(left, pltpu.roll(one, 64, axis=1), two)
    for q in range(8):
        res = by_lane(spread(gsrc[q, 0:1, :]), at_lane)
        for k in range(1, 8):
            res = jnp.where(at_row == k, by_lane(spread(gsrc[q, k : k + 1, :]), at_lane), res)
        gtab[q] = res
    for b in range(8):
        res = [jnp.zeros((8, LANES), F32), jnp.zeros((8, LANES), F32)]
        for z in range(PEERS):
            row = spread(recv_ref[z, :, 512 + LANES * b : 512 + LANES * b + LANES])
            for h in range(2):
                hit = idx_ref[8 * h : 8 * h + 8, :] == z
                res[h] = jnp.where(hit, by_lane(row, idx_ref[16 + 8 * h : 24 + 8 * h, :]), res[h])
        ytab[b, 0:8, :] = res[0]
        ytab[b, 8:16, :] = res[1]
    ends = []
    for g in range(SLOT_GROUPS):
        r1 = ends_ref[8 * g : 8 * g + 8, :]
        r2 = ends_ref[40 + 8 * g : 48 + 8 * g, :]
        dy = ends_ref[80 + 8 * g : 88 + 8 * g, :]
        ends.append((r1, r2, dy))
        for c in range(CHANS):
            for b in range(4):
                rows = slice(8 * ((2 * g + c) * 4 + b), 8 * ((2 * g + c) * 4 + b) + 8)
                table = gtab[2 * b + c]
                for r, dest in ((r1, la), (r2, lb)):
                    x = jnp.where((r & 3) == quad, by_sublane(table, r >> 2), 0.0)
                    x = x + pltpu.roll(x, 64, axis=1)
                    x = x + pltpu.roll(x, 32, axis=1)
                    hi, mid, lo = split3(x)
                    dest[rows, :] = jnp.where(quad == 0, hi, jnp.where(quad == 1, mid, lo))
                low = by_sublane(ytab[2 * b + c, 0:8, :], (dy >> 1) & 7)
                high = by_sublane(ytab[2 * b + c, 8:16, :], (dy >> 1) & 7)
                x = jnp.where((dy & 1) == half, jnp.where(dy < 16, low, high), 0.0)
                x = x + pltpu.roll(x, 64, axis=1)
                hi, mid, lo = split3(x)
                ly[rows, 0:128] = jnp.where(half == 0, hi, mid)
                ly[rows, 128:256] = lo
    ga[...] = jnp.dot(la[...].astype(BF16), e1_ref[...], preferred_element_type=F32)
    gb[...] = jnp.dot(lb[...].astype(BF16), e2_ref[...], preferred_element_type=F32)
    yy[...] = jnp.dot(ly[...].astype(BF16), ey_ref[...], preferred_element_type=F32)
    for g in range(SLOT_GROUPS):
        r1, r2, dy = ends[g]
        for c in range(CHANS):
            at_rows = [slice(8 * ((2 * g + c) * 4 + b), 8 * ((2 * g + c) * 4 + b) + 8) for b in range(4)]
            gbr, gbi, dbr, dbi = [gb[r, :] for r in at_rows]
            both = slice(16 * (2 * g + c), 16 * (2 * g + c) + 16)
            s_re = s_im = None
            for j in range(8):
                cols = slice(LANES * j, LANES * j + LANES)
                ga_r, ga_i, da_r, da_i = [ga[r, cols] for r in at_rows]
                y_r, y_i, t_r, t_i = [yy[r, cols] for r in at_rows]
                w = wts_ref[8 * g : 8 * g + 8, cols]
                p_r = ga_r * gbr + ga_i * gbi
                p_i = ga_i * gbr - ga_r * gbi
                q_r = (da_r * gbr + da_i * gbi) + (ga_r * dbr + ga_i * dbi)
                q_i = (da_i * gbr - da_r * gbi) + (ga_i * dbr - ga_r * dbi)
                u_r = w * ((q_r * y_r - q_i * y_i) + (p_r * t_r - p_i * t_i))
                u_i = w * ((q_r * y_i + q_i * y_r) + (p_r * t_i + p_i * t_r))
                v_r = u_r * y_r + u_i * y_i
                v_i = u_i * y_r - u_r * y_i
                f = jnp.concatenate([v_r * gbr - v_i * gbi, v_r * gbi + v_i * gbr], axis=0)
                a_r = v_r * ga_r + v_i * ga_i
                a_i = v_r * ga_i - v_i * ga_r
                d = jnp.concatenate([u_r * p_r + u_i * p_i, u_i * p_r - u_r * p_i], axis=0)
                for x, dest in ((f, xf), (d, xd)):
                    for k in range(PARTS):
                        part = x.astype(BF16)
                        dest[k, both, cols] = part
                        if k + 1 < PARTS:
                            x = x - part.astype(F32)
                s_re = a_r if j == 0 else s_re + a_r
                s_im = a_i if j == 0 else s_im + a_i
            for p, one in enumerate((s_re, s_im)):
                one = one + pltpu.roll(one, 64, axis=1)
                one = one + pltpu.roll(one, 32, axis=1)
                dest = slice(LANES * (2 * p + c), LANES * (2 * p + c + 1))
                ff[40 + 8 * g : 48 + 8 * g, dest] = jnp.where((r2 & 3) == quad, one, 0.0)
    first = jnp.dot(xf[0], s1_ref[...], preferred_element_type=F32)
    diag = jnp.dot(xd[0], sd_ref[...], preferred_element_type=F32)
    for k in range(1, PARTS):
        first = first + jnp.dot(xf[k], s1_ref[...], preferred_element_type=F32)
        diag = diag + jnp.dot(xd[k], sd_ref[...], preferred_element_type=F32)
    for g in range(SLOT_GROUPS):
        r1, r2, dy = ends[g]
        for c in range(CHANS):
            for p in range(2):
                rows = slice(16 * (2 * g + c) + 8 * p, 16 * (2 * g + c) + 8 * p + 8)
                dest = slice(LANES * (2 * p + c), LANES * (2 * p + c + 1))
                ff[8 * g : 8 * g + 8, dest] = jnp.where((r1 & 3) == quad, first[rows], 0.0)
                gg[8 * g : 8 * g + 8, dest] = jnp.where((dy & 1) == half, diag[rows], 0.0)
    gsum = ysum = None
    for fx, gx in zip(split3(ff[...]), split3(gg[...])):
        fk = jnp.dot(hot_ref[0:16, 0:80], fx.astype(BF16), preferred_element_type=F32)
        gk = jnp.dot(hot_ref[16:32, 0:40], gx.astype(BF16), preferred_element_type=F32)
        gsum = fk if gsum is None else gsum + fk
        ysum = gk if ysum is None else ysum + gk
    gout[...] = gsum[0:8]
    yout[...] = ysum
    at_row = idx_ref[32:40, :]
    at_lane = idx_ref[40:48, :]
    for p in range(2):
        res = []
        for c in range(CHANS):
            cols = slice(LANES * (2 * p + c), LANES * (2 * p + c + 1))
            one = by_lane(spread(gout[0:1, cols]), at_lane)
            for k in range(1, 8):
                one = jnp.where(at_row == k, by_lane(spread(gout[k : k + 1, cols]), at_lane), one)
            res.append(one)
        dest = slice(512 + LANES * p, 512 + LANES * (p + 1))
        out_ref[0:8, 0, dest] = jnp.where(left, res[0], pltpu.roll(res[1], 64, axis=1))
        out_ref[8:16, 0, dest] = jnp.where(left, pltpu.roll(res[0], 64, axis=1), res[1])
    for h in range(2):
        at_row = idx_ref[48 + 8 * h : 56 + 8 * h, :]
        at_lane = idx_ref[64 + 8 * h : 72 + 8 * h, :]
        for q in range(4):
            cols = slice(LANES * q, LANES * (q + 1))
            res = by_lane(spread(yout[0:1, cols]), at_lane)
            for k in range(1, 16):
                res = jnp.where(at_row == k, by_lane(spread(yout[k : k + 1, cols]), at_lane), res)
            out_ref[8 * h : 8 * h + 8, 0, cols] = res


def final_kernel(recv_ref, tan_ref, before_ref, after_ref, gain_ref, group_ref):
    for p in range(2):
        t0 = tan_ref[p, 0:1, :]
        t1 = tan_ref[p, 1:2, :]
        prior = [2.0 * t0 - before_ref[p] - t1, 2.0 * t1 - t0 - after_ref[p]]
        at = 512 + LANES * p
        total = recv_ref[0, :, at : at + LANES]
        for z in range(1, PEERS):
            total = total + recv_ref[z, :, at : at + LANES]
        for c in range(CHANS):
            gain_ref[p, c : c + 1, :] = total[:, 64 * c : 64 * c + 64] + PRIOR_WEIGHT * prior[c]
            at_q = LANES * (2 * p + c)
            sums = recv_ref[0, :, at_q : at_q + LANES]
            for z in range(1, PEERS):
                sums = sums + recv_ref[z, :, at_q : at_q + LANES]
            group_ref[p, c : c + 1, :] = sums[:, 0:GROUP_PART]


def near(x):
    return pltpu.with_memory_space_constraint(x, pltpu.VMEM)


def vmem(count):
    return [pl.BlockSpec(memory_space=pltpu.VMEM)] * count


def exchange(x):
    order = [[(LEAD + i * STEP) % PEERS for i in range(PEERS)]]
    return lax.all_to_all(x, "bl", 0, 0, axis_index_groups=order, tiled=True)


def local(gains, gain_tan, group_vis, group_tan, dish_of, group_of, block_list, weights):
    shape = jax.ShapeDtypeStruct
    sent = pl.pallas_call(
        pack_kernel,
        in_specs=vmem(4),
        out_specs=vmem(1)[0],
        out_shape=pltpu.VMEM((PEERS, 1, GATHER_WIDTH), F32),
        name="pack",
    )(gains, gain_tan, group_vis, group_tan)
    gathered = exchange(sent)
    peers = lax.axis_size("tf")
    up = [(i, i + 1) for i in range(peers - 1)]
    down = [(j, i) for i, j in up]
    before = lax.ppermute(gain_tan[:, 1:2], "tf", up)
    after = lax.ppermute(gain_tan[:, 0:1], "tf", down)
    dish_table = dish_of.reshape(8, LANES)
    group_table = jnp.pad(group_of, (0, 16 * LANES - GROUPS)).reshape(16, LANES)
    turned = jnp.pad(block_list.T, ((0, 0), (0, LANES - SLOTS)))
    tables = pl.pallas_call(
        prep_kernel,
        in_specs=vmem(5),
        out_specs=vmem(9),
        out_shape=(
            pltpu.VMEM((96, LANES), I32),
            pltpu.VMEM((120, LANES), I32),
            pltpu.VMEM((8 * SLOT_GROUPS, 1024), F32),
            pltpu.VMEM((32, LANES), BF16),
            pltpu.VMEM((LANES, 1024), BF16),
            pltpu.VMEM((LANES, LANES), BF16),
            pltpu.VMEM((2 * LANES, 1024), BF16),
            pltpu.VMEM((1024, LANES), BF16),
            pltpu.VMEM((1024, LANES), BF16),
        ),
        name="prep",
    )(dish_table, group_table, block_list, turned, weights)
    partial = pl.pallas_call(
        main_kernel,
        in_specs=vmem(10),
        out_specs=vmem(1)[0],
        out_shape=pltpu.VMEM((PEERS, 1, SCATTER_WIDTH), F32),
        scratch_shapes=[
            pltpu.VMEM((8, 8, LANES), F32),
            pltpu.VMEM((8, 8, LANES), F32),
            pltpu.VMEM((8, 16, LANES), F32),
            pltpu.VMEM((ROWS_ALL, LANES), F32),
            pltpu.VMEM((ROWS_ALL, LANES), F32),
            pltpu.VMEM((ROWS_ALL, 2 * LANES), F32),
            pltpu.VMEM((ROWS_ALL, 1024), F32),
            pltpu.VMEM((ROWS_ALL, LANES), F32),
            pltpu.VMEM((ROWS_ALL, 1024), F32),
            pltpu.VMEM((PARTS, ROWS_ALL // 2, 1024), BF16),
            pltpu.VMEM((PARTS, ROWS_ALL // 2, 1024), BF16),
            pltpu.VMEM((80, 4 * LANES), F32),
            pltpu.VMEM((40, 4 * LANES), F32),
            pltpu.VMEM((8, 4 * LANES), F32),
            pltpu.VMEM((16, 4 * LANES), F32),
        ],
        name="main",
    )(near(gathered), *[near(a) for a in tables])
    parts = exchange(partial)
    return pl.pallas_call(
        final_kernel,
        in_specs=vmem(4),
        out_specs=vmem(2),
        out_shape=(shape((2, CHANS, DISH_PART), F32), shape((2, CHANS, GROUP_PART), F32)),
        name="finish",
    )(near(parts), near(gain_tan), near(before), near(after))


def solution(mesh):
    placed = (
        P(None, "tf", "bl"),
        P(None, "tf", "bl"),
        P(None, "tf", "bl"),
        P(None, "tf", "bl"),
        P(),
        P(),
        P("bl", None),
        P("bl", None),
    )
    return jax.shard_map(
        local,
        mesh=mesh,
        in_specs=placed,
        out_specs=(P(None, "tf", "bl"), P(None, "tf", "bl")),
        check_vma=False,
    )
```

```python
import jax
import jax.numpy as jnp
from jax import lax
from jax.experimental import pallas as pl
from jax.experimental.pallas import tpu as pltpu
from jax.sharding import PartitionSpec as P

ROWS = 32
COLS = 32
DISHES = 1024
GROUPS = 1984
PRIOR_WEIGHT = 0.5

LANES = 128
PEERS = 16
DISH_PART = DISHES // PEERS
GROUP_PART = GROUPS // PEERS
CHANS = 2
SLOTS = 33
SLOT_GROUPS = 5
GATHER_WIDTH = 1536
SCATTER_WIDTH = 768
PARTS = 2
LEAD = 12
STEP = 1
UNSTEP = 1

F32 = jnp.float32
I32 = jnp.int32


def iota(shape, dim):
    return lax.broadcasted_iota(I32, shape, dim)


def by_lane(x, idx):
    return jnp.take_along_axis(x, idx, axis=1)


def by_sublane(x, idx):
    return jnp.take_along_axis(x, idx, axis=0)


def div124(g):
    return ((g >> 2) * 16913) >> 19


def div63(n):
    return (n * 66577) >> 22


def place(z):
    return ((z - LEAD) * UNSTEP) & (PEERS - 1)


def spread(row, rows=8):
    return jnp.broadcast_to(row, (rows, LANES))

BF16 = jnp.bfloat16
ROWS_ALL = 8 * 8 * SLOT_GROUPS


def split3(x):
    hi = x.astype(BF16).astype(F32)
    rest = x - hi
    mid = rest.astype(BF16).astype(F32)
    return hi, mid, rest - mid


def pack_kernel(gain_ref, tan_ref, vis_ref, gtan_ref, out_ref):
    for k, ref in enumerate((gain_ref, tan_ref)):
        for p in range(2):
            row = jnp.concatenate([ref[p, 0:1, :], ref[p, 1:2, :]], axis=1)
            at = LANES * (2 * k + p)
            out_ref[:, 0, at : at + LANES] = spread(row, PEERS)
    fill = jnp.zeros((1, LANES - GROUP_PART), F32)
    for k, ref in enumerate((vis_ref, gtan_ref)):
        for p in range(2):
            for c in range(CHANS):
                row = jnp.concatenate([ref[p, c : c + 1, :], fill], axis=1)
                at = 512 + LANES * (4 * k + 2 * p + c)
                out_ref[:, 0, at : at + LANES] = spread(row, PEERS)


def prep_kernel(
    dish_ref, group_ref, blocks_ref, turned_ref, weights_ref,
    idx_ref, ends_ref, wts_ref, hot_ref, e1_ref, e2_ref, ey_ref, s1_ref, sd_ref,
):
    lane = iota((8, LANES), 1)
    sub = iota((8, LANES), 0)
    for half in range(2):
        dy = 16 * half + 2 * sub + (lane >> 6)
        wrapped = lane & 63
        dx = jnp.where(wrapped < 32, wrapped, wrapped - 64)
        k = dy * 63 + dx - 1
        ok = (k >= 0) & (wrapped != 32)
        chunk = k >> 7
        at = k & 127
        first = (16 * half * 63 - 32) // 128
        last = ((16 * half + 15) * 63 + 31) // 128
        found = jnp.zeros((8, LANES), I32)
        for c in range(max(first, 0), min(last, 15) + 1):
            row = spread(group_ref[c : c + 1, :])
            found = jnp.where(chunk == c, by_lane(row, at), found)
        zg = div124(found)
        idx_ref[8 * half : 8 * half + 8, :] = jnp.where(ok, place(zg), -1)
        idx_ref[16 + 8 * half : 24 + 8 * half, :] = found - 124 * zg
    peer = iota((PEERS, LANES), 0)
    low = iota((LANES, LANES), 0)
    nt = (((1,), (1,)), ((), ()))
    acc = jnp.zeros((PEERS, LANES), F32)
    for c in range(8):
        ids = spread(dish_ref[c : c + 1, :])
        zone = place(ids >> 6)
        hot = sub == (zone & 7)
        left = jnp.concatenate(
            [jnp.where(hot, float(c), 0.0), jnp.where(hot, lane, 0).astype(F32)], axis=0
        )
        right = spread((ids & 63)[0:1] + 64 * (zone >> 3)[0:1], LANES) == low
        acc = acc + lax.dot_general(
            left.astype(BF16), right.astype(F32).astype(BF16), nt, preferred_element_type=F32
        )
    idx_ref[32:48, :] = (acc + 0.5).astype(I32)
    dish = dish_ref[...]
    zone = place(dish >> 6)
    idx_ref[80:88, :] = zone & 7
    idx_ref[88:96, :] = (dish & 63) + 64 * (zone >> 3)
    acc = jnp.zeros((2 * PEERS, LANES), F32)
    for c in range(16):
        ids = spread(group_ref[c : c + 1, :], PEERS)
        zone = div124(ids)
        n = LANES * c + iota((PEERS, LANES), 1)
        hot = (peer == place(zone)) & (n < GROUPS)
        dy = div63(n + 32)
        dx = n + 32 - 63 * dy - 31
        table_row = dy >> 1
        table_lane = 64 * (dy & 1) + (dx & 63)
        left = jnp.concatenate(
            [jnp.where(hot, table_row, 0), jnp.where(hot, table_lane, 0)], axis=0
        ).astype(F32)
        rest = (ids - 124 * zone)[0:1, :]
        right = spread(rest, LANES) == low
        acc = acc + lax.dot_general(
            left.astype(BF16), right.astype(F32).astype(BF16), nt, preferred_element_type=F32
        )
    idx_ref[48:80, :] = (acc + 0.5).astype(I32)
    for g in range(SLOT_GROUPS):
        pairs = blocks_ref[8 * g : 8 * g + 8, :] if g < 4 else blocks_ref[32:33, :]
        one = jnp.broadcast_to(pairs[:, 0:1], (8, LANES))
        two = jnp.broadcast_to(pairs[:, 1:2], (8, LANES))
        gap = two - one
        ends_ref[8 * g : 8 * g + 8, :] = one
        ends_ref[40 + 8 * g : 48 + 8 * g, :] = two
        ends_ref[80 + 8 * g : 88 + 8 * g, :] = gap
        for j in range(8):
            cols = slice(LANES * j, LANES * j + LANES)
            if g < 4:
                ok = (gap > 0) | ((lane & 31) > 4 * j + (lane >> 5))
                w = weights_ref[8 * g : 8 * g + 8, cols]
                wts_ref[8 * g : 8 * g + 8, cols] = jnp.where(ok, w.astype(F32), 0.0) * (1.0 / 32.0)
            else:
                ok = (gap > 0) | ((lane & 31) > 4 * sub + (lane >> 5))
                w = jnp.where(ok, spread(weights_ref[32:33, cols]).astype(F32), 0.0) * (1.0 / 32.0)
                wts_ref[32 + j : 33 + j, 0:LANES] = w[j : j + 1]
    lane16 = iota((PEERS, LANES), 1)
    one = spread(turned_ref[0:1, :], PEERS)
    two = spread(turned_ref[1:2, :], PEERS)
    ends = jnp.where(lane16 < 40, one, pltpu.roll(two, 40, axis=1))
    hot_ref[0:16, :] = jnp.where((ends >> 2) == peer, 1.0, 0.0).astype(BF16)
    hot_ref[16:32, :] = jnp.where(((two - one) >> 1) == peer, 1.0, 0.0).astype(BF16)
    k = iota((LANES, LANES), 0)
    l = iota((LANES, LANES), 1)
    e2_ref[0:128, :] = jnp.where(((k & 31) == (l & 31)) & (k < 96), 1.0, 0.0).astype(BF16)
    e2_ref[128:256, :] = jnp.where(((k & 3) == (l >> 5)) & (k < 96), 1.0, 0.0).astype(BF16)
    for j in range(8):
        cols = slice(LANES * j, LANES * j + LANES)
        c1 = 4 * j + (l >> 5)
        e1_ref[:, cols] = jnp.where(((k & 31) == c1) & (k < 96), 1.0, 0.0).astype(BF16)
        same = (k & 63) == (((l & 31) - c1) & 63)
        ey_ref[0:128, cols] = jnp.where(same, 1.0, 0.0).astype(BF16)
        ey_ref[128:256, cols] = jnp.where(same & (k < 64), 1.0, 0.0).astype(BF16)
        row1 = 4 * j + (k >> 5)
        s1_ref[cols, :] = jnp.where((l & 31) == row1, 1.0, 0.0).astype(BF16)
        sd_ref[cols, :] = jnp.where((l & 63) == (((k & 31) - row1) & 63), 1.0, 0.0).astype(BF16)


def main_kernel(
    recv_ref, idx_ref, ends_ref, wts_ref, hot_ref, e1_ref, e2_ref, ey_ref, s1_ref, sd_ref,
    out_ref,
    gsrc, gtab, ytab, la, lb, ly, ga, gb, yy, xf, xd, ff, gg, gout, yout,
):
    lane = iota((8, LANES), 1)
    quad = lane >> 5
    half = lane >> 6
    at_row = idx_ref[80:88, :]
    at_lane = idx_ref[88:96, :]
    left = half == 0
    for b in range(4):
        one = recv_ref[0:8, 0, LANES * b : LANES * b + LANES]
        two = recv_ref[8:16, 0, LANES * b : LANES * b + LANES]
        gsrc[2 * b] = jnp.where(left, one, pltpu.roll(two, 64, axis=1))
        gsrc[2 * b + 1] = jnp.where(left, pltpu.roll(one, 64, axis=1), two)
    for q in range(8):
        res = by_lane(spread(gsrc[q, 0:1, :]), at_lane)
        for k in range(1, 8):
            res = jnp.where(at_row == k, by_lane(spread(gsrc[q, k : k + 1, :]), at_lane), res)
        gtab[q] = res
    for b in range(8):
        res = [jnp.zeros((8, LANES), F32), jnp.zeros((8, LANES), F32)]
        for z in range(PEERS):
            row = spread(recv_ref[z, :, 512 + LANES * b : 512 + LANES * b + LANES])
            for h in range(2):
                hit = idx_ref[8 * h : 8 * h + 8, :] == z
                res[h] = jnp.where(hit, by_lane(row, idx_ref[16 + 8 * h : 24 + 8 * h, :]), res[h])
        ytab[b, 0:8, :] = res[0]
        ytab[b, 8:16, :] = res[1]
    def part_rows(g, c, k):
        at = 128 * k + 32 * g + 16 * c if g < 4 else 256 + 32 * k + 16 * c
        return slice(at, at + 16)

    def sums(rows, width, x, table):
        both = jnp.dot(x[rows, 0:width], table[0:width, :], preferred_element_type=F32)
        return both[0 : both.shape[0] // 2] + both[both.shape[0] // 2 :]

    sub = iota((8, LANES), 0)
    for g in range(SLOT_GROUPS):
        lone = g == SLOT_GROUPS - 1
        r1 = ends_ref[8 * g : 8 * g + 8, :]
        r2 = ends_ref[40 + 8 * g : 48 + 8 * g, :]
        dy = ends_ref[80 + 8 * g : 88 + 8 * g, :]
        for c in range(CHANS):
            for b in range(4):
                at = 64 * g + 32 * c + 8 * b
                rows = slice(at, at + 8)
                table = gtab[2 * b + c]
                for r, dest in ((r1, la), (r2, lb)):
                    x = jnp.where((r & 3) == quad, by_sublane(table, r >> 2), 0.0)
                    x = x + pltpu.roll(x, 64, axis=1)
                    x = x + pltpu.roll(x, 32, axis=1)
                    if lone and dest is la:
                        x = jnp.where(((lane >> 2) & 7) == sub, x, 0.0)
                    hi, mid, lo = split3(x)
                    dest[rows, :] = jnp.where(quad == 0, hi, jnp.where(quad == 1, mid, lo))
                low = by_sublane(ytab[2 * b + c, 0:8, :], (dy >> 1) & 7)
                high = by_sublane(ytab[2 * b + c, 8:16, :], (dy >> 1) & 7)
                x = jnp.where((dy & 1) == half, jnp.where(dy < 16, low, high), 0.0)
                x = x + pltpu.roll(x, 64, axis=1)
                if lone:
                    x = pltpu.roll(x, 0, axis=1, stride=4, stride_axis=0)
                hi, mid, lo = split3(x)
                ly[rows, 0:128] = jnp.where(half == 0, hi, mid)
                ly[rows, 128:256] = lo
    full, last = slice(0, 256), slice(256, 320)
    gb[...] = jnp.dot(lb[...].astype(BF16), e2_ref[0:128, :], preferred_element_type=F32)
    ga[full, :] = jnp.dot(la[full, :].astype(BF16), e1_ref[...], preferred_element_type=F32)
    yy[full, :] = jnp.dot(ly[full, :].astype(BF16), ey_ref[...], preferred_element_type=F32)
    ga[last, 0:LANES] = jnp.dot(la[last, :].astype(BF16), e2_ref[128:256, :], preferred_element_type=F32)
    yy[last, 0:LANES] = jnp.dot(ly[last, :].astype(BF16), ey_ref[:, 0:LANES], preferred_element_type=F32)
    for g in range(SLOT_GROUPS):
        lone = g == SLOT_GROUPS - 1
        r2 = ends_ref[40 + 8 * g : 48 + 8 * g, :]
        for c in range(CHANS):
            at_rows = [slice(64 * g + 32 * c + 8 * b, 64 * g + 32 * c + 8 * b + 8) for b in range(4)]
            gbr, gbi, dbr, dbi = [gb[r, :] for r in at_rows]
            s_re = s_im = None
            for j in range(1 if lone else 8):
                cols = slice(LANES * j, LANES * j + LANES)
                ga_r, ga_i, da_r, da_i = [ga[r, cols] for r in at_rows]
                y_r, y_i, t_r, t_i = [yy[r, cols] for r in at_rows]
                w = wts_ref[8 * g : 8 * g + 8, cols]
                p_r = ga_r * gbr + ga_i * gbi
                p_i = ga_i * gbr - ga_r * gbi
                q_r = (da_r * gbr + da_i * gbi) + (ga_r * dbr + ga_i * dbi)
                q_i = (da_i * gbr - da_r * gbi) + (ga_i * dbr - ga_r * dbi)
                u_r = w * ((q_r * y_r - q_i * y_i) + (p_r * t_r - p_i * t_i))
                u_i = w * ((q_r * y_i + q_i * y_r) + (p_r * t_i + p_i * t_r))
                v_r = u_r * y_r + u_i * y_i
                v_i = u_i * y_r - u_r * y_i
                f = jnp.concatenate([v_r * gbr - v_i * gbi, v_r * gbi + v_i * gbr], axis=0)
                a_r = v_r * ga_r + v_i * ga_i
                a_i = v_r * ga_i - v_i * ga_r
                d = jnp.concatenate([u_r * p_r + u_i * p_i, u_i * p_r - u_r * p_i], axis=0)
                for x, dest in ((f, xf), (d, xd)):
                    for k in range(PARTS):
                        part = x.astype(BF16)
                        dest[part_rows(g, c, k), cols] = part
                        if k + 1 < PARTS:
                            x = x - part.astype(F32)
                s_re = a_r if j == 0 else s_re + a_r
                s_im = a_i if j == 0 else s_im + a_i
            for p, one in enumerate((s_re, s_im)):
                one = one + pltpu.roll(one, 64, axis=1)
                one = one + pltpu.roll(one, 32, axis=1)
                dest = slice(LANES * (2 * p + c), LANES * (2 * p + c + 1))
                ff[40 + 8 * g : 48 + 8 * g, dest] = jnp.where((r2 & 3) == quad, one, 0.0)
    first = [sums(slice(0, 256), 1024, xf, s1_ref), sums(slice(256, 320), LANES, xf, s1_ref)]
    diag = [sums(slice(0, 256), 1024, xd, sd_ref), sums(slice(256, 320), LANES, xd, sd_ref)]
    for g in range(SLOT_GROUPS):
        r1 = ends_ref[8 * g : 8 * g + 8, :]
        dy = ends_ref[80 + 8 * g : 88 + 8 * g, :]
        for c in range(CHANS):
            for p in range(2):
                at = 32 * (g % 4) + 16 * c + 8 * p
                dest = slice(LANES * (2 * p + c), LANES * (2 * p + c + 1))
                f, d = first[g // 4][at : at + 8], diag[g // 4][at : at + 8]
                if g == SLOT_GROUPS - 1:
                    f = pltpu.roll(f, 0, axis=1, stride=4, stride_axis=0)
                    for bit in (1, 2, 4):
                        d = jnp.where((sub & bit) != 0, pltpu.roll(d, 64 - 4 * bit, axis=1), d)
                ff[8 * g : 8 * g + 8, dest] = jnp.where((r1 & 3) == quad, f, 0.0)
                gg[8 * g : 8 * g + 8, dest] = jnp.where((dy & 1) == half, d, 0.0)
    gsum = ysum = None
    for fx, gx in zip(split3(ff[...]), split3(gg[...])):
        fk = jnp.dot(hot_ref[0:16, 0:80], fx.astype(BF16), preferred_element_type=F32)
        gk = jnp.dot(hot_ref[16:32, 0:40], gx.astype(BF16), preferred_element_type=F32)
        gsum = fk if gsum is None else gsum + fk
        ysum = gk if ysum is None else ysum + gk
    gout[...] = gsum[0:8]
    yout[...] = ysum
    at_row = idx_ref[32:40, :]
    at_lane = idx_ref[40:48, :]
    for p in range(2):
        res = []
        for c in range(CHANS):
            cols = slice(LANES * (2 * p + c), LANES * (2 * p + c + 1))
            one = by_lane(spread(gout[0:1, cols]), at_lane)
            for k in range(1, 8):
                one = jnp.where(at_row == k, by_lane(spread(gout[k : k + 1, cols]), at_lane), one)
            res.append(one)
        dest = slice(512 + LANES * p, 512 + LANES * (p + 1))
        out_ref[0:8, 0, dest] = jnp.where(left, res[0], pltpu.roll(res[1], 64, axis=1))
        out_ref[8:16, 0, dest] = jnp.where(left, pltpu.roll(res[0], 64, axis=1), res[1])
    for h in range(2):
        at_row = idx_ref[48 + 8 * h : 56 + 8 * h, :]
        at_lane = idx_ref[64 + 8 * h : 72 + 8 * h, :]
        for q in range(4):
            cols = slice(LANES * q, LANES * (q + 1))
            res = by_lane(spread(yout[0:1, cols]), at_lane)
            for k in range(1, 16):
                res = jnp.where(at_row == k, by_lane(spread(yout[k : k + 1, cols]), at_lane), res)
            out_ref[8 * h : 8 * h + 8, 0, cols] = res


def final_kernel(recv_ref, tan_ref, before_ref, after_ref, gain_ref, group_ref):
    for p in range(2):
        t0 = tan_ref[p, 0:1, :]
        t1 = tan_ref[p, 1:2, :]
        prior = [2.0 * t0 - before_ref[p] - t1, 2.0 * t1 - t0 - after_ref[p]]
        at = 512 + LANES * p
        total = recv_ref[0, :, at : at + LANES]
        for z in range(1, PEERS):
            total = total + recv_ref[z, :, at : at + LANES]
        for c in range(CHANS):
            gain_ref[p, c : c + 1, :] = total[:, 64 * c : 64 * c + 64] + PRIOR_WEIGHT * prior[c]
            at_q = LANES * (2 * p + c)
            sums = recv_ref[0, :, at_q : at_q + LANES]
            for z in range(1, PEERS):
                sums = sums + recv_ref[z, :, at_q : at_q + LANES]
            group_ref[p, c : c + 1, :] = sums[:, 0:GROUP_PART]


def near(x):
    return pltpu.with_memory_space_constraint(x, pltpu.VMEM)


def vmem(count):
    return [pl.BlockSpec(memory_space=pltpu.VMEM)] * count


def exchange(x):
    order = [[(LEAD + i * STEP) % PEERS for i in range(PEERS)]]
    return lax.all_to_all(x, "bl", 0, 0, axis_index_groups=order, tiled=True)


def local(gains, gain_tan, group_vis, group_tan, dish_of, group_of, block_list, weights):
    shape = jax.ShapeDtypeStruct
    sent = pl.pallas_call(
        pack_kernel,
        in_specs=vmem(4),
        out_specs=vmem(1)[0],
        out_shape=pltpu.VMEM((PEERS, 1, GATHER_WIDTH), F32),
        name="pack",
    )(gains, gain_tan, group_vis, group_tan)
    gathered = exchange(sent)
    peers = lax.axis_size("tf")
    up = [(i, i + 1) for i in range(peers - 1)]
    down = [(j, i) for i, j in up]
    before = lax.ppermute(gain_tan[:, 1:2], "tf", up)
    after = lax.ppermute(gain_tan[:, 0:1], "tf", down)
    dish_table = dish_of.reshape(8, LANES)
    group_table = jnp.pad(group_of, (0, 16 * LANES - GROUPS)).reshape(16, LANES)
    turned = jnp.pad(block_list.T, ((0, 0), (0, LANES - SLOTS)), mode="edge")
    tables = pl.pallas_call(
        prep_kernel,
        in_specs=vmem(5),
        out_specs=vmem(9),
        out_shape=(
            pltpu.VMEM((96, LANES), I32),
            pltpu.VMEM((120, LANES), I32),
            pltpu.VMEM((8 * SLOT_GROUPS, 1024), F32),
            pltpu.VMEM((32, LANES), BF16),
            pltpu.VMEM((LANES, 1024), BF16),
            pltpu.VMEM((2 * LANES, LANES), BF16),
            pltpu.VMEM((2 * LANES, 1024), BF16),
            pltpu.VMEM((1024, LANES), BF16),
            pltpu.VMEM((1024, LANES), BF16),
        ),
        name="prep",
    )(dish_table, group_table, block_list, turned, weights)
    partial = pl.pallas_call(
        main_kernel,
        in_specs=vmem(10),
        out_specs=vmem(1)[0],
        out_shape=pltpu.VMEM((PEERS, 1, SCATTER_WIDTH), F32),
        scratch_shapes=[
            pltpu.VMEM((8, 8, LANES), F32),
            pltpu.VMEM((8, 8, LANES), F32),
            pltpu.VMEM((8, 16, LANES), F32),
            pltpu.VMEM((ROWS_ALL, LANES), F32),
            pltpu.VMEM((ROWS_ALL, LANES), F32),
            pltpu.VMEM((ROWS_ALL, 2 * LANES), F32),
            pltpu.VMEM((ROWS_ALL, 1024), F32),
            pltpu.VMEM((ROWS_ALL, LANES), F32),
            pltpu.VMEM((ROWS_ALL, 1024), F32),
            pltpu.VMEM((PARTS * ROWS_ALL // 2, 1024), BF16),
            pltpu.VMEM((PARTS * ROWS_ALL // 2, 1024), BF16),
            pltpu.VMEM((80, 4 * LANES), F32),
            pltpu.VMEM((40, 4 * LANES), F32),
            pltpu.VMEM((8, 4 * LANES), F32),
            pltpu.VMEM((16, 4 * LANES), F32),
        ],
        name="main",
    )(near(gathered), *[near(a) for a in tables])
    parts = exchange(partial)
    return pl.pallas_call(
        final_kernel,
        in_specs=vmem(4),
        out_specs=vmem(2),
        out_shape=(shape((2, CHANS, DISH_PART), F32), shape((2, CHANS, GROUP_PART), F32)),
        name="finish",
    )(near(parts), near(gain_tan), near(before), near(after))


def solution(mesh):
    placed = (
        P(None, "tf", "bl"),
        P(None, "tf", "bl"),
        P(None, "tf", "bl"),
        P(None, "tf", "bl"),
        P(),
        P(),
        P("bl", None),
        P("bl", None),
    )
    return jax.shard_map(
        local,
        mesh=mesh,
        in_specs=placed,
        out_specs=(P(None, "tf", "bl"), P(None, "tf", "bl")),
        check_vma=False,
    )
```

```python
import jax
import jax.numpy as jnp
from jax import lax
from jax.experimental import pallas as pl
from jax.experimental.pallas import tpu as pltpu
from jax.sharding import PartitionSpec as P

ROWS = 32
COLS = 32
DISHES = 1024
GROUPS = 1984
PRIOR_WEIGHT = 0.5

LANES = 128
PEERS = 16
DISH_PART = DISHES // PEERS
GROUP_PART = GROUPS // PEERS
CHANS = 2
SLOTS = 33
SLOT_GROUPS = 5
GATHER_WIDTH = 1536
SCATTER_WIDTH = 768
PARTS = 2
LEAD = 12
STEP = 1
UNSTEP = 1

F32 = jnp.float32
I32 = jnp.int32


def iota(shape, dim):
    return lax.broadcasted_iota(I32, shape, dim)


def by_lane(x, idx):
    return jnp.take_along_axis(x, idx, axis=1)


def by_sublane(x, idx):
    return jnp.take_along_axis(x, idx, axis=0)


def div124(g):
    return ((g >> 2) * 16913) >> 19


def div63(n):
    return (n * 66577) >> 22


def place(z):
    return ((z - LEAD) * UNSTEP) & (PEERS - 1)


def spread(row, rows=8):
    return jnp.broadcast_to(row, (rows, LANES))

BF16 = jnp.bfloat16
ROWS_ALL = 8 * 8 * SLOT_GROUPS


def split3(x):
    hi = x.astype(BF16).astype(F32)
    rest = x - hi
    mid = rest.astype(BF16).astype(F32)
    return hi, mid, rest - mid


def pack_kernel(gain_ref, tan_ref, vis_ref, gtan_ref, out_ref):
    for k, ref in enumerate((gain_ref, tan_ref)):
        for p in range(2):
            row = jnp.concatenate([ref[p, 0:1, :], ref[p, 1:2, :]], axis=1)
            at = LANES * (2 * k + p)
            out_ref[:, 0, at : at + LANES] = spread(row, PEERS)
    fill = jnp.zeros((1, LANES - GROUP_PART), F32)
    for k, ref in enumerate((vis_ref, gtan_ref)):
        for p in range(2):
            for c in range(CHANS):
                row = jnp.concatenate([ref[p, c : c + 1, :], fill], axis=1)
                at = 512 + LANES * (4 * k + 2 * p + c)
                out_ref[:, 0, at : at + LANES] = spread(row, PEERS)


def prep_kernel(
    dish_ref, group_ref, blocks_ref, turned_ref, weights_ref,
    idx_ref, ends_ref, wts_ref, hot_ref, e1_ref, e2_ref, ey_ref, s1_ref, sd_ref, pick_ref,
):
    lane = iota((8, LANES), 1)
    sub = iota((8, LANES), 0)
    for half in range(2):
        dy = 16 * half + 2 * sub + (lane >> 6)
        wrapped = lane & 63
        dx = jnp.where(wrapped < 32, wrapped, wrapped - 64)
        k = dy * 63 + dx - 1
        ok = (k >= 0) & (wrapped != 32)
        chunk = k >> 7
        at = k & 127
        first = (16 * half * 63 - 32) // 128
        last = ((16 * half + 15) * 63 + 31) // 128
        found = jnp.zeros((8, LANES), I32)
        for c in range(max(first, 0), min(last, 15) + 1):
            row = spread(group_ref[c : c + 1, :])
            found = jnp.where(chunk == c, by_lane(row, at), found)
        zg = div124(found)
        idx_ref[8 * half : 8 * half + 8, :] = jnp.where(ok, place(zg), -1)
        idx_ref[16 + 8 * half : 24 + 8 * half, :] = found - 124 * zg
    for r in range(16):
        take = spread(idx_ref[16 + r : 17 + r, :], LANES) == iota((LANES, LANES), 0)
        take = jnp.where(take, 1.0, 0.0).astype(BF16)
        for part in range(2):
            pick_ref[LANES * part : LANES * part + LANES, LANES * r : LANES * r + LANES] = take
    peer = iota((PEERS, LANES), 0)
    low = iota((LANES, LANES), 0)
    nt = (((1,), (1,)), ((), ()))
    acc = jnp.zeros((PEERS, LANES), F32)
    for c in range(8):
        ids = spread(dish_ref[c : c + 1, :])
        zone = place(ids >> 6)
        hot = sub == (zone & 7)
        left = jnp.concatenate(
            [jnp.where(hot, float(c), 0.0), jnp.where(hot, lane, 0).astype(F32)], axis=0
        )
        right = spread((ids & 63)[0:1] + 64 * (zone >> 3)[0:1], LANES) == low
        acc = acc + lax.dot_general(
            left.astype(BF16), right.astype(F32).astype(BF16), nt, preferred_element_type=F32
        )
    idx_ref[32:48, :] = (acc + 0.5).astype(I32)
    dish = dish_ref[...]
    zone = place(dish >> 6)
    idx_ref[80:88, :] = zone & 7
    idx_ref[88:96, :] = (dish & 63) + 64 * (zone >> 3)
    acc = jnp.zeros((2 * PEERS, LANES), F32)
    for c in range(16):
        ids = spread(group_ref[c : c + 1, :], PEERS)
        zone = div124(ids)
        n = LANES * c + iota((PEERS, LANES), 1)
        hot = (peer == place(zone)) & (n < GROUPS)
        dy = div63(n + 32)
        dx = n + 32 - 63 * dy - 31
        table_row = dy >> 1
        table_lane = 64 * (dy & 1) + (dx & 63)
        left = jnp.concatenate(
            [jnp.where(hot, table_row, 0), jnp.where(hot, table_lane, 0)], axis=0
        ).astype(F32)
        rest = (ids - 124 * zone)[0:1, :]
        right = spread(rest, LANES) == low
        acc = acc + lax.dot_general(
            left.astype(BF16), right.astype(F32).astype(BF16), nt, preferred_element_type=F32
        )
    idx_ref[48:80, :] = (acc + 0.5).astype(I32)
    for g in range(SLOT_GROUPS):
        pairs = blocks_ref[8 * g : 8 * g + 8, :] if g < 4 else blocks_ref[32:33, :]
        one = jnp.broadcast_to(pairs[:, 0:1], (8, LANES))
        two = jnp.broadcast_to(pairs[:, 1:2], (8, LANES))
        gap = two - one
        ends_ref[8 * g : 8 * g + 8, :] = one
        ends_ref[40 + 8 * g : 48 + 8 * g, :] = two
        ends_ref[80 + 8 * g : 88 + 8 * g, :] = gap
        for j in range(8):
            cols = slice(LANES * j, LANES * j + LANES)
            if g < 4:
                ok = (gap > 0) | ((lane & 31) > 4 * j + (lane >> 5))
                w = weights_ref[8 * g : 8 * g + 8, cols]
                wts_ref[8 * g : 8 * g + 8, cols] = jnp.where(ok, w.astype(F32), 0.0) * (1.0 / 32.0)
            else:
                ok = (gap > 0) | ((lane & 31) > 4 * sub + (lane >> 5))
                w = jnp.where(ok, spread(weights_ref[32:33, cols]).astype(F32), 0.0) * (1.0 / 32.0)
                wts_ref[32 + j : 33 + j, 0:LANES] = w[j : j + 1]
    lane16 = iota((PEERS, LANES), 1)
    one = spread(turned_ref[0:1, :], PEERS)
    two = spread(turned_ref[1:2, :], PEERS)
    ends = jnp.where(lane16 < 40, one, pltpu.roll(two, 40, axis=1))
    hot_ref[0:16, :] = jnp.where((ends >> 2) == peer, 1.0, 0.0).astype(BF16)
    hot_ref[16:32, :] = jnp.where(((two - one) >> 1) == peer, 1.0, 0.0).astype(BF16)
    k = iota((LANES, LANES), 0)
    l = iota((LANES, LANES), 1)
    e2_ref[0:128, :] = jnp.where(((k & 31) == (l & 31)) & (k < 96), 1.0, 0.0).astype(BF16)
    e2_ref[128:256, :] = jnp.where(((k & 3) == (l >> 5)) & (k < 96), 1.0, 0.0).astype(BF16)
    for j in range(8):
        cols = slice(LANES * j, LANES * j + LANES)
        c1 = 4 * j + (l >> 5)
        e1_ref[:, cols] = jnp.where(((k & 31) == c1) & (k < 96), 1.0, 0.0).astype(BF16)
        same = (k & 63) == (((l & 31) - c1) & 63)
        ey_ref[0:128, cols] = jnp.where(same, 1.0, 0.0).astype(BF16)
        ey_ref[128:256, cols] = jnp.where(same & (k < 64), 1.0, 0.0).astype(BF16)
        row1 = 4 * j + (k >> 5)
        s1_ref[cols, :] = jnp.where((l & 31) == row1, 1.0, 0.0).astype(BF16)
        sd_ref[cols, :] = jnp.where((l & 63) == (((k & 31) - row1) & 63), 1.0, 0.0).astype(BF16)


def main_kernel(
    recv_ref, idx_ref, ends_ref, wts_ref, hot_ref, e1_ref, e2_ref, ey_ref, s1_ref, sd_ref, pick_ref,
    out_ref,
    lx, taken, gsrc, gtab, ytab, la, lb, ly, ga, gb, yy, xf, xd, ff, gg, gout, yout,
):
    lane = iota((8, LANES), 1)
    quad = lane >> 5
    half = lane >> 6
    at_row = idx_ref[80:88, :]
    at_lane = idx_ref[88:96, :]
    left = half == 0
    for b in range(4):
        one = recv_ref[0:8, 0, LANES * b : LANES * b + LANES]
        two = recv_ref[8:16, 0, LANES * b : LANES * b + LANES]
        gsrc[2 * b] = jnp.where(left, one, pltpu.roll(two, 64, axis=1))
        gsrc[2 * b + 1] = jnp.where(left, pltpu.roll(one, 64, axis=1), two)
    for q in range(8):
        res = by_lane(spread(gsrc[q, 0:1, :]), at_lane)
        for k in range(1, 8):
            res = jnp.where(at_row == k, by_lane(spread(gsrc[q, k : k + 1, :]), at_lane), res)
        gtab[q] = res
    for q in range(8):
        x = recv_ref[:, 0, 512 + LANES * q : 512 + LANES * q + LANES]
        part = x.astype(BF16)
        lx[16 * q : 16 * q + 16, 0:128] = part
        lx[16 * q : 16 * q + 16, 128:256] = (x - part.astype(F32)).astype(BF16)
    taken[...] = jnp.dot(lx[...], pick_ref[...], preferred_element_type=F32)
    peer = iota((PEERS, LANES), 0)
    for r in range(16):
        hit = spread(idx_ref[r : r + 1, :], PEERS) == peer
        for q in range(8):
            x = jnp.where(hit, taken[16 * q : 16 * q + 16, LANES * r : LANES * r + LANES], 0.0)
            ytab[q, r : r + 1, :] = jnp.sum(x, axis=0, keepdims=True)
    def part_rows(g, c, k):
        at = 128 * k + 32 * g + 16 * c if g < 4 else 256 + 32 * k + 16 * c
        return slice(at, at + 16)

    def sums(rows, width, x, table):
        both = jnp.dot(x[rows, 0:width], table[0:width, :], preferred_element_type=F32)
        return both[0 : both.shape[0] // 2] + both[both.shape[0] // 2 :]

    sub = iota((8, LANES), 0)
    for g in range(SLOT_GROUPS):
        lone = g == SLOT_GROUPS - 1
        r1 = ends_ref[8 * g : 8 * g + 8, :]
        r2 = ends_ref[40 + 8 * g : 48 + 8 * g, :]
        dy = ends_ref[80 + 8 * g : 88 + 8 * g, :]
        for c in range(CHANS):
            for b in range(4):
                at = 64 * g + 32 * c + 8 * b
                rows = slice(at, at + 8)
                table = gtab[2 * b + c]
                for r, dest in ((r1, la), (r2, lb)):
                    x = jnp.where((r & 3) == quad, by_sublane(table, r >> 2), 0.0)
                    x = x + pltpu.roll(x, 64, axis=1)
                    x = x + pltpu.roll(x, 32, axis=1)
                    if lone and dest is la:
                        x = jnp.where(((lane >> 2) & 7) == sub, x, 0.0)
                    hi, mid, lo = split3(x)
                    dest[rows, :] = jnp.where(quad == 0, hi, jnp.where(quad == 1, mid, lo))
                low = by_sublane(ytab[2 * b + c, 0:8, :], (dy >> 1) & 7)
                high = by_sublane(ytab[2 * b + c, 8:16, :], (dy >> 1) & 7)
                x = jnp.where((dy & 1) == half, jnp.where(dy < 16, low, high), 0.0)
                x = x + pltpu.roll(x, 64, axis=1)
                if lone:
                    x = pltpu.roll(x, 0, axis=1, stride=4, stride_axis=0)
                hi, mid, lo = split3(x)
                ly[rows, 0:128] = jnp.where(half == 0, hi, mid)
                ly[rows, 128:256] = lo
    full, last = slice(0, 256), slice(256, 320)
    gb[...] = jnp.dot(lb[...].astype(BF16), e2_ref[0:128, :], preferred_element_type=F32)
    ga[full, :] = jnp.dot(la[full, :].astype(BF16), e1_ref[...], preferred_element_type=F32)
    yy[full, :] = jnp.dot(ly[full, :].astype(BF16), ey_ref[...], preferred_element_type=F32)
    ga[last, 0:LANES] = jnp.dot(la[last, :].astype(BF16), e2_ref[128:256, :], preferred_element_type=F32)
    yy[last, 0:LANES] = jnp.dot(ly[last, :].astype(BF16), ey_ref[:, 0:LANES], preferred_element_type=F32)
    for g in range(SLOT_GROUPS):
        lone = g == SLOT_GROUPS - 1
        r2 = ends_ref[40 + 8 * g : 48 + 8 * g, :]
        for c in range(CHANS):
            at_rows = [slice(64 * g + 32 * c + 8 * b, 64 * g + 32 * c + 8 * b + 8) for b in range(4)]
            gbr, gbi, dbr, dbi = [gb[r, :] for r in at_rows]
            s_re = s_im = None
            for j in range(1 if lone else 8):
                cols = slice(LANES * j, LANES * j + LANES)
                ga_r, ga_i, da_r, da_i = [ga[r, cols] for r in at_rows]
                y_r, y_i, t_r, t_i = [yy[r, cols] for r in at_rows]
                w = wts_ref[8 * g : 8 * g + 8, cols]
                p_r = ga_r * gbr + ga_i * gbi
                p_i = ga_i * gbr - ga_r * gbi
                q_r = (da_r * gbr + da_i * gbi) + (ga_r * dbr + ga_i * dbi)
                q_i = (da_i * gbr - da_r * gbi) + (ga_i * dbr - ga_r * dbi)
                u_r = w * ((q_r * y_r - q_i * y_i) + (p_r * t_r - p_i * t_i))
                u_i = w * ((q_r * y_i + q_i * y_r) + (p_r * t_i + p_i * t_r))
                v_r = u_r * y_r + u_i * y_i
                v_i = u_i * y_r - u_r * y_i
                f = jnp.concatenate([v_r * gbr - v_i * gbi, v_r * gbi + v_i * gbr], axis=0)
                a_r = v_r * ga_r + v_i * ga_i
                a_i = v_r * ga_i - v_i * ga_r
                d = jnp.concatenate([u_r * p_r + u_i * p_i, u_i * p_r - u_r * p_i], axis=0)
                for x, dest in ((f, xf), (d, xd)):
                    for k in range(PARTS):
                        part = x.astype(BF16)
                        dest[part_rows(g, c, k), cols] = part
                        if k + 1 < PARTS:
                            x = x - part.astype(F32)
                s_re = a_r if j == 0 else s_re + a_r
                s_im = a_i if j == 0 else s_im + a_i
            for p, one in enumerate((s_re, s_im)):
                one = one + pltpu.roll(one, 64, axis=1)
                one = one + pltpu.roll(one, 32, axis=1)
                dest = slice(LANES * (2 * p + c), LANES * (2 * p + c + 1))
                ff[40 + 8 * g : 48 + 8 * g, dest] = jnp.where((r2 & 3) == quad, one, 0.0)
    first = [sums(slice(0, 256), 1024, xf, s1_ref), sums(slice(256, 320), LANES, xf, s1_ref)]
    diag = [sums(slice(0, 256), 1024, xd, sd_ref), sums(slice(256, 320), LANES, xd, sd_ref)]
    for g in range(SLOT_GROUPS):
        r1 = ends_ref[8 * g : 8 * g + 8, :]
        dy = ends_ref[80 + 8 * g : 88 + 8 * g, :]
        for c in range(CHANS):
            for p in range(2):
                at = 32 * (g % 4) + 16 * c + 8 * p
                dest = slice(LANES * (2 * p + c), LANES * (2 * p + c + 1))
                f, d = first[g // 4][at : at + 8], diag[g // 4][at : at + 8]
                if g == SLOT_GROUPS - 1:
                    f = pltpu.roll(f, 0, axis=1, stride=4, stride_axis=0)
                    for bit in (1, 2, 4):
                        d = jnp.where((sub & bit) != 0, pltpu.roll(d, 64 - 4 * bit, axis=1), d)
                ff[8 * g : 8 * g + 8, dest] = jnp.where((r1 & 3) == quad, f, 0.0)
                gg[8 * g : 8 * g + 8, dest] = jnp.where((dy & 1) == half, d, 0.0)
    gsum = ysum = None
    for fx, gx in zip(split3(ff[...]), split3(gg[...])):
        fk = jnp.dot(hot_ref[0:16, 0:80], fx.astype(BF16), preferred_element_type=F32)
        gk = jnp.dot(hot_ref[16:32, 0:40], gx.astype(BF16), preferred_element_type=F32)
        gsum = fk if gsum is None else gsum + fk
        ysum = gk if ysum is None else ysum + gk
    gout[...] = gsum[0:8]
    yout[...] = ysum
    at_row = idx_ref[32:40, :]
    at_lane = idx_ref[40:48, :]
    for p in range(2):
        res = []
        for c in range(CHANS):
            cols = slice(LANES * (2 * p + c), LANES * (2 * p + c + 1))
            one = by_lane(spread(gout[0:1, cols]), at_lane)
            for k in range(1, 8):
                one = jnp.where(at_row == k, by_lane(spread(gout[k : k + 1, cols]), at_lane), one)
            res.append(one)
        dest = slice(512 + LANES * p, 512 + LANES * (p + 1))
        out_ref[0:8, 0, dest] = jnp.where(left, res[0], pltpu.roll(res[1], 64, axis=1))
        out_ref[8:16, 0, dest] = jnp.where(left, pltpu.roll(res[0], 64, axis=1), res[1])
    for h in range(2):
        at_row = idx_ref[48 + 8 * h : 56 + 8 * h, :]
        at_lane = idx_ref[64 + 8 * h : 72 + 8 * h, :]
        for q in range(4):
            cols = slice(LANES * q, LANES * (q + 1))
            res = by_lane(spread(yout[0:1, cols]), at_lane)
            for k in range(1, 16):
                res = jnp.where(at_row == k, by_lane(spread(yout[k : k + 1, cols]), at_lane), res)
            out_ref[8 * h : 8 * h + 8, 0, cols] = res


def final_kernel(recv_ref, tan_ref, before_ref, after_ref, gain_ref, group_ref):
    for p in range(2):
        t0 = tan_ref[p, 0:1, :]
        t1 = tan_ref[p, 1:2, :]
        prior = [2.0 * t0 - before_ref[p] - t1, 2.0 * t1 - t0 - after_ref[p]]
        at = 512 + LANES * p
        total = recv_ref[0, :, at : at + LANES]
        for z in range(1, PEERS):
            total = total + recv_ref[z, :, at : at + LANES]
        for c in range(CHANS):
            gain_ref[p, c : c + 1, :] = total[:, 64 * c : 64 * c + 64] + PRIOR_WEIGHT * prior[c]
            at_q = LANES * (2 * p + c)
            sums = recv_ref[0, :, at_q : at_q + LANES]
            for z in range(1, PEERS):
                sums = sums + recv_ref[z, :, at_q : at_q + LANES]
            group_ref[p, c : c + 1, :] = sums[:, 0:GROUP_PART]


def near(x):
    return pltpu.with_memory_space_constraint(x, pltpu.VMEM)


def vmem(count):
    return [pl.BlockSpec(memory_space=pltpu.VMEM)] * count


def exchange(x):
    order = [[(LEAD + i * STEP) % PEERS for i in range(PEERS)]]
    return lax.all_to_all(x, "bl", 0, 0, axis_index_groups=order, tiled=True)


def local(gains, gain_tan, group_vis, group_tan, dish_of, group_of, block_list, weights):
    shape = jax.ShapeDtypeStruct
    sent = pl.pallas_call(
        pack_kernel,
        in_specs=vmem(4),
        out_specs=vmem(1)[0],
        out_shape=pltpu.VMEM((PEERS, 1, GATHER_WIDTH), F32),
        name="pack",
    )(gains, gain_tan, group_vis, group_tan)
    gathered = exchange(sent)
    peers = lax.axis_size("tf")
    up = [(i, i + 1) for i in range(peers - 1)]
    down = [(j, i) for i, j in up]
    before = lax.ppermute(gain_tan[:, 1:2], "tf", up)
    after = lax.ppermute(gain_tan[:, 0:1], "tf", down)
    dish_table = dish_of.reshape(8, LANES)
    group_table = jnp.pad(group_of, (0, 16 * LANES - GROUPS)).reshape(16, LANES)
    turned = jnp.pad(block_list.T, ((0, 0), (0, LANES - SLOTS)), mode="edge")
    tables = pl.pallas_call(
        prep_kernel,
        in_specs=vmem(5),
        out_specs=vmem(10),
        out_shape=(
            pltpu.VMEM((96, LANES), I32),
            pltpu.VMEM((120, LANES), I32),
            pltpu.VMEM((8 * SLOT_GROUPS, 1024), F32),
            pltpu.VMEM((32, LANES), BF16),
            pltpu.VMEM((LANES, 1024), BF16),
            pltpu.VMEM((2 * LANES, LANES), BF16),
            pltpu.VMEM((2 * LANES, 1024), BF16),
            pltpu.VMEM((1024, LANES), BF16),
            pltpu.VMEM((1024, LANES), BF16),
            pltpu.VMEM((2 * LANES, 16 * LANES), BF16),
        ),
        name="prep",
    )(dish_table, group_table, block_list, turned, weights)
    partial = pl.pallas_call(
        main_kernel,
        in_specs=vmem(11),
        out_specs=vmem(1)[0],
        out_shape=pltpu.VMEM((PEERS, 1, SCATTER_WIDTH), F32),
        scratch_shapes=[
            pltpu.VMEM((LANES, 2 * LANES), BF16),
            pltpu.VMEM((LANES, 16 * LANES), F32),
            pltpu.VMEM((8, 8, LANES), F32),
            pltpu.VMEM((8, 8, LANES), F32),
            pltpu.VMEM((8, 16, LANES), F32),
            pltpu.VMEM((ROWS_ALL, LANES), F32),
            pltpu.VMEM((ROWS_ALL, LANES), F32),
            pltpu.VMEM((ROWS_ALL, 2 * LANES), F32),
            pltpu.VMEM((ROWS_ALL, 1024), F32),
            pltpu.VMEM((ROWS_ALL, LANES), F32),
            pltpu.VMEM((ROWS_ALL, 1024), F32),
            pltpu.VMEM((PARTS * ROWS_ALL // 2, 1024), BF16),
            pltpu.VMEM((PARTS * ROWS_ALL // 2, 1024), BF16),
            pltpu.VMEM((80, 4 * LANES), F32),
            pltpu.VMEM((40, 4 * LANES), F32),
            pltpu.VMEM((8, 4 * LANES), F32),
            pltpu.VMEM((16, 4 * LANES), F32),
        ],
        name="main",
    )(near(gathered), *[near(a) for a in tables])
    parts = exchange(partial)
    return pl.pallas_call(
        final_kernel,
        in_specs=vmem(4),
        out_specs=vmem(2),
        out_shape=(shape((2, CHANS, DISH_PART), F32), shape((2, CHANS, GROUP_PART), F32)),
        name="finish",
    )(near(parts), near(gain_tan), near(before), near(after))


def solution(mesh):
    placed = (
        P(None, "tf", "bl"),
        P(None, "tf", "bl"),
        P(None, "tf", "bl"),
        P(None, "tf", "bl"),
        P(),
        P(),
        P("bl", None),
        P("bl", None),
    )
    return jax.shard_map(
        local,
        mesh=mesh,
        in_specs=placed,
        out_specs=(P(None, "tf", "bl"), P(None, "tf", "bl")),
        check_vma=False,
    )
```

```python
import jax
import jax.numpy as jnp
from jax import lax
from jax.experimental import pallas as pl
from jax.experimental.pallas import tpu as pltpu
from jax.sharding import PartitionSpec as P

ROWS = 32
COLS = 32
DISHES = 1024
GROUPS = 1984
PRIOR_WEIGHT = 0.5

LANES = 128
PEERS = 16
DISH_PART = DISHES // PEERS
GROUP_PART = GROUPS // PEERS
CHANS = 2
SLOTS = 33
SLOT_GROUPS = 5
GATHER_WIDTH = 1536
SCATTER_WIDTH = 768
PARTS = 2
LEAD = 13
STEP = 1
UNSTEP = 1

F32 = jnp.float32
I32 = jnp.int32


def iota(shape, dim):
    return lax.broadcasted_iota(I32, shape, dim)


def by_lane(x, idx):
    return jnp.take_along_axis(x, idx, axis=1)


def by_sublane(x, idx):
    return jnp.take_along_axis(x, idx, axis=0)


def div124(g):
    return ((g >> 2) * 16913) >> 19


def div63(n):
    return (n * 66577) >> 22


def place(z):
    return ((z - LEAD) * UNSTEP) & (PEERS - 1)


def spread(row, rows=8):
    return jnp.broadcast_to(row, (rows, LANES))

BF16 = jnp.bfloat16
ROWS_ALL = 8 * 8 * SLOT_GROUPS


def split3(x):
    hi = x.astype(BF16).astype(F32)
    rest = x - hi
    mid = rest.astype(BF16).astype(F32)
    return hi, mid, rest - mid


def pack_kernel(gain_ref, tan_ref, vis_ref, gtan_ref, out_ref):
    for k, ref in enumerate((gain_ref, tan_ref)):
        for p in range(2):
            row = jnp.concatenate([ref[p, 0:1, :], ref[p, 1:2, :]], axis=1)
            at = LANES * (2 * k + p)
            out_ref[:, 0, at : at + LANES] = spread(row, PEERS)
    fill = jnp.zeros((1, LANES - GROUP_PART), F32)
    for k, ref in enumerate((vis_ref, gtan_ref)):
        for p in range(2):
            for c in range(CHANS):
                row = jnp.concatenate([ref[p, c : c + 1, :], fill], axis=1)
                at = 512 + LANES * (4 * k + 2 * p + c)
                out_ref[:, 0, at : at + LANES] = spread(row, PEERS)


def prep_kernel(
    dish_ref, group_ref, blocks_ref, turned_ref, weights_ref,
    idx_ref, ends_ref, wts_ref, hot_ref, e1_ref, e2_ref, ey_ref, s1_ref, sd_ref, pick_ref,
):
    lane = iota((8, LANES), 1)
    sub = iota((8, LANES), 0)
    for half in range(2):
        dy = 16 * half + 2 * sub + (lane >> 6)
        wrapped = lane & 63
        dx = jnp.where(wrapped < 32, wrapped, wrapped - 64)
        k = dy * 63 + dx - 1
        ok = (k >= 0) & (wrapped != 32)
        chunk = k >> 7
        at = k & 127
        first = (16 * half * 63 - 32) // 128
        last = ((16 * half + 15) * 63 + 31) // 128
        found = jnp.zeros((8, LANES), I32)
        for c in range(max(first, 0), min(last, 15) + 1):
            row = spread(group_ref[c : c + 1, :])
            found = jnp.where(chunk == c, by_lane(row, at), found)
        zg = div124(found)
        idx_ref[8 * half : 8 * half + 8, :] = jnp.where(ok, place(zg), -1)
        idx_ref[16 + 8 * half : 24 + 8 * half, :] = found - 124 * zg
    for r in range(16):
        take = spread(idx_ref[16 + r : 17 + r, :], LANES) == iota((LANES, LANES), 0)
        take = jnp.where(take, 1.0, 0.0).astype(BF16)
        for part in range(2):
            pick_ref[LANES * part : LANES * part + LANES, LANES * r : LANES * r + LANES] = take
    peer = iota((PEERS, LANES), 0)
    low = iota((LANES, LANES), 0)
    nt = (((1,), (1,)), ((), ()))
    acc = jnp.zeros((PEERS, LANES), F32)
    for c in range(8):
        ids = spread(dish_ref[c : c + 1, :])
        zone = place(ids >> 6)
        hot = sub == (zone & 7)
        left = jnp.concatenate(
            [jnp.where(hot, float(c), 0.0), jnp.where(hot, lane, 0).astype(F32)], axis=0
        )
        right = spread((ids & 63)[0:1] + 64 * (zone >> 3)[0:1], LANES) == low
        acc = acc + lax.dot_general(
            left.astype(BF16), right.astype(F32).astype(BF16), nt, preferred_element_type=F32
        )
    idx_ref[32:48, :] = (acc + 0.5).astype(I32)
    dish = dish_ref[...]
    zone = place(dish >> 6)
    idx_ref[80:88, :] = zone & 7
    idx_ref[88:96, :] = (dish & 63) + 64 * (zone >> 3)
    acc = jnp.zeros((2 * PEERS, LANES), F32)
    for c in range(16):
        ids = spread(group_ref[c : c + 1, :], PEERS)
        zone = div124(ids)
        n = LANES * c + iota((PEERS, LANES), 1)
        hot = (peer == place(zone)) & (n < GROUPS)
        dy = div63(n + 32)
        dx = n + 32 - 63 * dy - 31
        table_row = dy >> 1
        table_lane = 64 * (dy & 1) + (dx & 63)
        left = jnp.concatenate(
            [jnp.where(hot, table_row, 0), jnp.where(hot, table_lane, 0)], axis=0
        ).astype(F32)
        rest = (ids - 124 * zone)[0:1, :]
        right = spread(rest, LANES) == low
        acc = acc + lax.dot_general(
            left.astype(BF16), right.astype(F32).astype(BF16), nt, preferred_element_type=F32
        )
    idx_ref[48:80, :] = (acc + 0.5).astype(I32)
    for g in range(SLOT_GROUPS):
        pairs = blocks_ref[8 * g : 8 * g + 8, :] if g < 4 else blocks_ref[32:33, :]
        one = jnp.broadcast_to(pairs[:, 0:1], (8, LANES))
        two = jnp.broadcast_to(pairs[:, 1:2], (8, LANES))
        gap = two - one
        ends_ref[8 * g : 8 * g + 8, :] = one
        ends_ref[40 + 8 * g : 48 + 8 * g, :] = two
        ends_ref[80 + 8 * g : 88 + 8 * g, :] = gap
        for j in range(8):
            cols = slice(LANES * j, LANES * j + LANES)
            if g < 4:
                ok = (gap > 0) | ((lane & 31) > 4 * j + (lane >> 5))
                w = weights_ref[8 * g : 8 * g + 8, cols]
                wts_ref[8 * g : 8 * g + 8, cols] = jnp.where(ok, w.astype(F32), 0.0) * (1.0 / 32.0)
            else:
                ok = (gap > 0) | ((lane & 31) > 4 * sub + (lane >> 5))
                w = jnp.where(ok, spread(weights_ref[32:33, cols]).astype(F32), 0.0) * (1.0 / 32.0)
                wts_ref[32 + j : 33 + j, 0:LANES] = w[j : j + 1]
    lane16 = iota((PEERS, LANES), 1)
    one = spread(turned_ref[0:1, :], PEERS)
    two = spread(turned_ref[1:2, :], PEERS)
    ends = jnp.where(lane16 < 40, one, pltpu.roll(two, 40, axis=1))
    hot_ref[0:16, :] = jnp.where((ends >> 2) == peer, 1.0, 0.0).astype(BF16)
    hot_ref[16:32, :] = jnp.where(((two - one) >> 1) == peer, 1.0, 0.0).astype(BF16)
    k = iota((LANES, LANES), 0)
    l = iota((LANES, LANES), 1)
    e2_ref[0:128, :] = jnp.where(((k & 31) == (l & 31)) & (k < 96), 1.0, 0.0).astype(BF16)
    e2_ref[128:256, :] = jnp.where(((k & 3) == (l >> 5)) & (k < 96), 1.0, 0.0).astype(BF16)
    for j in range(8):
        cols = slice(LANES * j, LANES * j + LANES)
        c1 = 4 * j + (l >> 5)
        e1_ref[:, cols] = jnp.where(((k & 31) == c1) & (k < 96), 1.0, 0.0).astype(BF16)
        same = (k & 63) == (((l & 31) - c1) & 63)
        ey_ref[0:128, cols] = jnp.where(same, 1.0, 0.0).astype(BF16)
        ey_ref[128:256, cols] = jnp.where(same & (k < 64), 1.0, 0.0).astype(BF16)
        row1 = 4 * j + (k >> 5)
        s1_ref[cols, :] = jnp.where((l & 31) == row1, 1.0, 0.0).astype(BF16)
        sd_ref[cols, :] = jnp.where((l & 63) == (((k & 31) - row1) & 63), 1.0, 0.0).astype(BF16)


def main_kernel(
    recv_ref, idx_ref, ends_ref, wts_ref, hot_ref, e1_ref, e2_ref, ey_ref, s1_ref, sd_ref, pick_ref,
    out_ref,
    lx, taken, gsrc, gtab, ytab, la, lb, ly, ga, gb, yy, xf, xd, ff, gg, gout, yout,
):
    lane = iota((8, LANES), 1)
    quad = lane >> 5
    half = lane >> 6
    at_row = idx_ref[80:88, :]
    at_lane = idx_ref[88:96, :]
    left = half == 0
    for b in range(4):
        one = recv_ref[0:8, 0, LANES * b : LANES * b + LANES]
        two = recv_ref[8:16, 0, LANES * b : LANES * b + LANES]
        gsrc[2 * b] = jnp.where(left, one, pltpu.roll(two, 64, axis=1))
        gsrc[2 * b + 1] = jnp.where(left, pltpu.roll(one, 64, axis=1), two)
    for q in range(8):
        res = by_lane(spread(gsrc[q, 0:1, :]), at_lane)
        for k in range(1, 8):
            res = jnp.where(at_row == k, by_lane(spread(gsrc[q, k : k + 1, :]), at_lane), res)
        gtab[q] = res
    for q in range(8):
        x = recv_ref[:, 0, 512 + LANES * q : 512 + LANES * q + LANES]
        part = x.astype(BF16)
        lx[16 * q : 16 * q + 16, 0:128] = part
        lx[16 * q : 16 * q + 16, 128:256] = (x - part.astype(F32)).astype(BF16)
    taken[...] = jnp.dot(lx[...], pick_ref[...], preferred_element_type=F32)
    peer = iota((PEERS, LANES), 0)
    for r in range(16):
        hit = spread(idx_ref[r : r + 1, :], PEERS) == peer
        for q in range(8):
            x = jnp.where(hit, taken[16 * q : 16 * q + 16, LANES * r : LANES * r + LANES], 0.0)
            ytab[q, r : r + 1, :] = jnp.sum(x, axis=0, keepdims=True)
    def part_rows(g, c, k):
        at = 128 * k + 32 * g + 16 * c if g < 4 else 256 + 32 * k + 16 * c
        return slice(at, at + 16)

    def sums(rows, width, x, table):
        both = jnp.dot(x[rows, 0:width], table[0:width, :], preferred_element_type=F32)
        return both[0 : both.shape[0] // 2] + both[both.shape[0] // 2 :]

    sub = iota((8, LANES), 0)
    for g in range(SLOT_GROUPS):
        lone = g == SLOT_GROUPS - 1
        r1 = ends_ref[8 * g : 8 * g + 8, :]
        r2 = ends_ref[40 + 8 * g : 48 + 8 * g, :]
        dy = ends_ref[80 + 8 * g : 88 + 8 * g, :]
        for c in range(CHANS):
            for b in range(4):
                at = 64 * g + 32 * c + 8 * b
                rows = slice(at, at + 8)
                table = gtab[2 * b + c]
                for r, dest in ((r1, la), (r2, lb)):
                    x = jnp.where((r & 3) == quad, by_sublane(table, r >> 2), 0.0)
                    x = x + pltpu.roll(x, 64, axis=1)
                    x = x + pltpu.roll(x, 32, axis=1)
                    if lone and dest is la:
                        x = jnp.where(((lane >> 2) & 7) == sub, x, 0.0)
                    hi, mid, lo = split3(x)
                    dest[rows, :] = jnp.where(quad == 0, hi, jnp.where(quad == 1, mid, lo))
                low = by_sublane(ytab[2 * b + c, 0:8, :], (dy >> 1) & 7)
                high = by_sublane(ytab[2 * b + c, 8:16, :], (dy >> 1) & 7)
                x = jnp.where((dy & 1) == half, jnp.where(dy < 16, low, high), 0.0)
                x = x + pltpu.roll(x, 64, axis=1)
                if lone:
                    x = pltpu.roll(x, 0, axis=1, stride=4, stride_axis=0)
                hi, mid, lo = split3(x)
                ly[rows, 0:128] = jnp.where(half == 0, hi, mid)
                ly[rows, 128:256] = lo
    full, last = slice(0, 256), slice(256, 320)
    gb[...] = jnp.dot(lb[...].astype(BF16), e2_ref[0:128, :], preferred_element_type=F32)
    ga[full, :] = jnp.dot(la[full, :].astype(BF16), e1_ref[...], preferred_element_type=F32)
    yy[full, :] = jnp.dot(ly[full, :].astype(BF16), ey_ref[...], preferred_element_type=F32)
    ga[last, 0:LANES] = jnp.dot(la[last, :].astype(BF16), e2_ref[128:256, :], preferred_element_type=F32)
    yy[last, 0:LANES] = jnp.dot(ly[last, :].astype(BF16), ey_ref[:, 0:LANES], preferred_element_type=F32)
    for g in range(SLOT_GROUPS):
        lone = g == SLOT_GROUPS - 1
        r2 = ends_ref[40 + 8 * g : 48 + 8 * g, :]
        for c in range(CHANS):
            at_rows = [slice(64 * g + 32 * c + 8 * b, 64 * g + 32 * c + 8 * b + 8) for b in range(4)]
            gbr, gbi, dbr, dbi = [gb[r, :] for r in at_rows]
            s_re = s_im = None
            for j in range(1 if lone else 8):
                cols = slice(LANES * j, LANES * j + LANES)
                ga_r, ga_i, da_r, da_i = [ga[r, cols] for r in at_rows]
                y_r, y_i, t_r, t_i = [yy[r, cols] for r in at_rows]
                w = wts_ref[8 * g : 8 * g + 8, cols]
                p_r = ga_r * gbr + ga_i * gbi
                p_i = ga_i * gbr - ga_r * gbi
                q_r = (da_r * gbr + da_i * gbi) + (ga_r * dbr + ga_i * dbi)
                q_i = (da_i * gbr - da_r * gbi) + (ga_i * dbr - ga_r * dbi)
                u_r = w * ((q_r * y_r - q_i * y_i) + (p_r * t_r - p_i * t_i))
                u_i = w * ((q_r * y_i + q_i * y_r) + (p_r * t_i + p_i * t_r))
                v_r = u_r * y_r + u_i * y_i
                v_i = u_i * y_r - u_r * y_i
                f = jnp.concatenate([v_r * gbr - v_i * gbi, v_r * gbi + v_i * gbr], axis=0)
                a_r = v_r * ga_r + v_i * ga_i
                a_i = v_r * ga_i - v_i * ga_r
                d = jnp.concatenate([u_r * p_r + u_i * p_i, u_i * p_r - u_r * p_i], axis=0)
                for x, dest in ((f, xf), (d, xd)):
                    for k in range(PARTS):
                        part = x.astype(BF16)
                        dest[part_rows(g, c, k), cols] = part
                        if k + 1 < PARTS:
                            x = x - part.astype(F32)
                s_re = a_r if j == 0 else s_re + a_r
                s_im = a_i if j == 0 else s_im + a_i
            for p, one in enumerate((s_re, s_im)):
                one = one + pltpu.roll(one, 64, axis=1)
                one = one + pltpu.roll(one, 32, axis=1)
                dest = slice(LANES * (2 * p + c), LANES * (2 * p + c + 1))
                ff[40 + 8 * g : 48 + 8 * g, dest] = jnp.where((r2 & 3) == quad, one, 0.0)
    first = [sums(slice(0, 256), 1024, xf, s1_ref), sums(slice(256, 320), LANES, xf, s1_ref)]
    diag = [sums(slice(0, 256), 1024, xd, sd_ref), sums(slice(256, 320), LANES, xd, sd_ref)]
    for g in range(SLOT_GROUPS):
        r1 = ends_ref[8 * g : 8 * g + 8, :]
        dy = ends_ref[80 + 8 * g : 88 + 8 * g, :]
        for c in range(CHANS):
            for p in range(2):
                at = 32 * (g % 4) + 16 * c + 8 * p
                dest = slice(LANES * (2 * p + c), LANES * (2 * p + c + 1))
                f, d = first[g // 4][at : at + 8], diag[g // 4][at : at + 8]
                if g == SLOT_GROUPS - 1:
                    f = pltpu.roll(f, 0, axis=1, stride=4, stride_axis=0)
                    for bit in (1, 2, 4):
                        d = jnp.where((sub & bit) != 0, pltpu.roll(d, 64 - 4 * bit, axis=1), d)
                ff[8 * g : 8 * g + 8, dest] = jnp.where((r1 & 3) == quad, f, 0.0)
                gg[8 * g : 8 * g + 8, dest] = jnp.where((dy & 1) == half, d, 0.0)
    gsum = ysum = None
    for fx, gx in zip(split3(ff[...]), split3(gg[...])):
        fk = jnp.dot(hot_ref[0:16, 0:80], fx.astype(BF16), preferred_element_type=F32)
        gk = jnp.dot(hot_ref[16:32, 0:40], gx.astype(BF16), preferred_element_type=F32)
        gsum = fk if gsum is None else gsum + fk
        ysum = gk if ysum is None else ysum + gk
    gout[...] = gsum[0:8]
    yout[...] = ysum
    at_row = idx_ref[32:40, :]
    at_lane = idx_ref[40:48, :]
    for p in range(2):
        res = []
        for c in range(CHANS):
            cols = slice(LANES * (2 * p + c), LANES * (2 * p + c + 1))
            one = by_lane(spread(gout[0:1, cols]), at_lane)
            for k in range(1, 8):
                one = jnp.where(at_row == k, by_lane(spread(gout[k : k + 1, cols]), at_lane), one)
            res.append(one)
        dest = slice(512 + LANES * p, 512 + LANES * (p + 1))
        out_ref[0:8, 0, dest] = jnp.where(left, res[0], pltpu.roll(res[1], 64, axis=1))
        out_ref[8:16, 0, dest] = jnp.where(left, pltpu.roll(res[0], 64, axis=1), res[1])
    for h in range(2):
        at_row = idx_ref[48 + 8 * h : 56 + 8 * h, :]
        at_lane = idx_ref[64 + 8 * h : 72 + 8 * h, :]
        for q in range(4):
            cols = slice(LANES * q, LANES * (q + 1))
            res = by_lane(spread(yout[0:1, cols]), at_lane)
            for k in range(1, 16):
                res = jnp.where(at_row == k, by_lane(spread(yout[k : k + 1, cols]), at_lane), res)
            out_ref[8 * h : 8 * h + 8, 0, cols] = res


def final_kernel(recv_ref, tan_ref, before_ref, after_ref, gain_ref, group_ref):
    for p in range(2):
        t0 = tan_ref[p, 0:1, :]
        t1 = tan_ref[p, 1:2, :]
        prior = [2.0 * t0 - before_ref[p] - t1, 2.0 * t1 - t0 - after_ref[p]]
        at = 512 + LANES * p
        total = recv_ref[0, :, at : at + LANES]
        for z in range(1, PEERS):
            total = total + recv_ref[z, :, at : at + LANES]
        for c in range(CHANS):
            gain_ref[p, c : c + 1, :] = total[:, 64 * c : 64 * c + 64] + PRIOR_WEIGHT * prior[c]
            at_q = LANES * (2 * p + c)
            sums = recv_ref[0, :, at_q : at_q + LANES]
            for z in range(1, PEERS):
                sums = sums + recv_ref[z, :, at_q : at_q + LANES]
            group_ref[p, c : c + 1, :] = sums[:, 0:GROUP_PART]


def near(x):
    return pltpu.with_memory_space_constraint(x, pltpu.VMEM)


def vmem(count):
    return [pl.BlockSpec(memory_space=pltpu.VMEM)] * count


def exchange(x):
    order = [[(LEAD + i * STEP) % PEERS for i in range(PEERS)]]
    return lax.all_to_all(x, "bl", 0, 0, axis_index_groups=order, tiled=True)


def local(gains, gain_tan, group_vis, group_tan, dish_of, group_of, block_list, weights):
    shape = jax.ShapeDtypeStruct
    sent = pl.pallas_call(
        pack_kernel,
        in_specs=vmem(4),
        out_specs=vmem(1)[0],
        out_shape=pltpu.VMEM((PEERS, 1, GATHER_WIDTH), F32),
        name="pack",
    )(gains, gain_tan, group_vis, group_tan)
    gathered = exchange(sent)
    peers = lax.axis_size("tf")
    up = [(i, i + 1) for i in range(peers - 1)]
    down = [(j, i) for i, j in up]
    before = lax.ppermute(gain_tan[:, 1:2], "tf", up)
    after = lax.ppermute(gain_tan[:, 0:1], "tf", down)
    dish_table = dish_of.reshape(8, LANES)
    group_table = jnp.pad(group_of, (0, 16 * LANES - GROUPS)).reshape(16, LANES)
    turned = jnp.pad(block_list.T, ((0, 0), (0, LANES - SLOTS)), mode="edge")
    tables = pl.pallas_call(
        prep_kernel,
        in_specs=vmem(5),
        out_specs=vmem(10),
        out_shape=(
            pltpu.VMEM((96, LANES), I32),
            pltpu.VMEM((120, LANES), I32),
            pltpu.VMEM((8 * SLOT_GROUPS, 1024), F32),
            pltpu.VMEM((32, LANES), BF16),
            pltpu.VMEM((LANES, 1024), BF16),
            pltpu.VMEM((2 * LANES, LANES), BF16),
            pltpu.VMEM((2 * LANES, 1024), BF16),
            pltpu.VMEM((1024, LANES), BF16),
            pltpu.VMEM((1024, LANES), BF16),
            pltpu.VMEM((2 * LANES, 16 * LANES), BF16),
        ),
        name="prep",
    )(dish_table, group_table, block_list, turned, weights)
    partial = pl.pallas_call(
        main_kernel,
        in_specs=vmem(11),
        out_specs=vmem(1)[0],
        out_shape=pltpu.VMEM((PEERS, 1, SCATTER_WIDTH), F32),
        scratch_shapes=[
            pltpu.VMEM((LANES, 2 * LANES), BF16),
            pltpu.VMEM((LANES, 16 * LANES), F32),
            pltpu.VMEM((8, 8, LANES), F32),
            pltpu.VMEM((8, 8, LANES), F32),
            pltpu.VMEM((8, 16, LANES), F32),
            pltpu.VMEM((ROWS_ALL, LANES), F32),
            pltpu.VMEM((ROWS_ALL, LANES), F32),
            pltpu.VMEM((ROWS_ALL, 2 * LANES), F32),
            pltpu.VMEM((ROWS_ALL, 1024), F32),
            pltpu.VMEM((ROWS_ALL, LANES), F32),
            pltpu.VMEM((ROWS_ALL, 1024), F32),
            pltpu.VMEM((PARTS * ROWS_ALL // 2, 1024), BF16),
            pltpu.VMEM((PARTS * ROWS_ALL // 2, 1024), BF16),
            pltpu.VMEM((80, 4 * LANES), F32),
            pltpu.VMEM((40, 4 * LANES), F32),
            pltpu.VMEM((8, 4 * LANES), F32),
            pltpu.VMEM((16, 4 * LANES), F32),
        ],
        name="main",
    )(near(gathered), *[near(a) for a in tables])
    parts = exchange(partial)
    return pl.pallas_call(
        final_kernel,
        in_specs=vmem(4),
        out_specs=vmem(2),
        out_shape=(shape((2, CHANS, DISH_PART), F32), shape((2, CHANS, GROUP_PART), F32)),
        name="finish",
    )(near(parts), near(gain_tan), near(before), near(after))


def solution(mesh):
    placed = (
        P(None, "tf", "bl"),
        P(None, "tf", "bl"),
        P(None, "tf", "bl"),
        P(None, "tf", "bl"),
        P(),
        P(),
        P("bl", None),
        P("bl", None),
    )
    return jax.shard_map(
        local,
        mesh=mesh,
        in_specs=placed,
        out_specs=(P(None, "tf", "bl"), P(None, "tf", "bl")),
        check_vma=False,
    )
```
